128 devices in a mesh: pipe: 4 (over y), dp: 4 (over z_hi, core), tensor: 8 (over z_lo, x).
Axes of the slice: x: 4, y: 4, z: 4 (z_hi: 2, z_lo: 2; z = z_hi * 2 + z_lo), core: 2. Of those that a mesh axis runs over, the one named last changes fastest.
Arguments:
- output_gradient: bfloat16 [16, 128, 8192], P('dp', None, 'tensor'), may hold values from -6 to 6
- acts: bfloat16 [16, 4, 128, 8192], P('dp', 'pipe', None, 'tensor'), may hold values from -6 to 6
- weights: bfloat16 [4, 8192, 8192], P('pipe', 'tensor'), may hold values from -0.0625 to 0.0625
- adapter_down_factors: bfloat16 [4, 8192, 128], P('pipe', 'tensor'), may hold values from -0.0625 to 0.0625
- adapter_up_factors: bfloat16 [4, 128, 8192], P('pipe'), may hold values from -0.0625 to 0.0625
- feature_sign_bits: int32 [8192, 64], replicated, may hold values from 0 to 1
- rank_sign_bits: int32 [128, 128], replicated, may hold values from 0 to 1
- lengths: int32 [16], P('dp'), may hold values from 32 to 128, as said below
Outputs:
- features: float32 [16, 4, 8192], P('dp', 'pipe', 'tensor')
The draws below stay inside these ranges and needn't reach their ends.
Inputs may be any that keep to these rules, and one draw needn't show every extreme that they name: `lengths`: the first example has exactly 128 real tokens.
All inputs are finite; a program needn't handle non-finite values.
Results may differ from the reference program's by a relative error of at most 0.0065.
Values may be sent and summed in bfloat16 or wider, within the bound.
A program may use at most 128 MiB of HBM per device.

```python
import math
import jax
import jax.numpy as jnp
from jax import lax

MODEL_WIDTH = 8192
ADAPTER_RANK = 128
PROJ = 64
LEN = 128
SECTION_COUNT = 4
EXAMPLES = 16


def draw_lengths(key, part):
    values = jax.random.randint(key, (EXAMPLES,), LEN // 4, LEN + 1)
    return values.at[0].set(LEN).astype(jnp.int32)


def with_ends(entries, rng, low, largest):
    place = [jax.random.randint(jax.random.fold_in(rng, axis), (), 0, length) for axis, length in enumerate(entries.shape)]
    longest = entries.shape.index(max(entries.shape))
    neighbour = place[:longest] + [(place[longest] + 1) % entries.shape[longest]] + place[longest + 1:]
    return entries.at[tuple(place)].set(low).at[tuple(neighbour)].set(largest)


def steps_of(key, shape, pieces, least, largest):
    level = 1.0
    for position, blocks in pieces:
        heights = jax.random.uniform(jax.random.fold_in(jax.random.fold_in(key, 6), position), (blocks,), jnp.float32, least / len(pieces), largest / len(pieces))
        level = level * jnp.repeat(jnp.exp(heights), shape[position] // blocks).reshape((-1,) + (1,) * (len(shape) - 1 - position))
    return level


def noise(stream_key, shape, deviation, reach, split=(), held_as=jnp.bfloat16):
    gain = steps_of(stream_key, shape, split, -0.22, 0.18) if split else 1.0
    drawn = jax.random.normal(stream_key, shape, jnp.float32) * deviation * gain
    return jnp.minimum(jnp.maximum(drawn, -reach), reach).astype(held_as)


def setup_inputs(seed: int = 0) -> dict:
    key_list = jax.random.split(jax.random.key(seed), 9)
    output_gradient = noise(key_list[0], (EXAMPLES, LEN, MODEL_WIDTH), 1.0, 6.0, ((0, 4), (2, 8)))
    acts = noise(key_list[1], (EXAMPLES, SECTION_COUNT, LEN, MODEL_WIDTH), 1.0, 6.0, ((0, 4), (1, 4), (3, 8)))
    weights = noise(key_list[2], (SECTION_COUNT, MODEL_WIDTH, MODEL_WIDTH), MODEL_WIDTH ** -0.5, 0.0625, ((0, 4), (1, 8)))
    adapter_down_factors = noise(key_list[3], (SECTION_COUNT, MODEL_WIDTH, ADAPTER_RANK), MODEL_WIDTH ** -0.5, 0.0625, ((0, 4), (1, 8)))
    adapter_up_factors = noise(key_list[4], (SECTION_COUNT, ADAPTER_RANK, MODEL_WIDTH), MODEL_WIDTH ** -0.5, 0.0625, ((0, 4),))
    feature_sign_bits = with_ends(jax.random.randint(key_list[5], (MODEL_WIDTH, PROJ), 0, 2), jax.random.fold_in(key_list[5], 1), 0, 1).astype(jnp.int32)
    rank_sign_bits = with_ends(jax.random.randint(key_list[6], (ADAPTER_RANK, 2 * PROJ), 0, 2), jax.random.fold_in(key_list[6], 1), 0, 1).astype(jnp.int32)
    lengths = draw_lengths(jax.random.fold_in(key_list[8], 71), 0)
    return {"output_gradient": output_gradient, "acts": acts, "weights": weights, "adapter_down_factors": adapter_down_factors, "adapter_up_factors": adapter_up_factors, "feature_sign_bits": feature_sign_bits, "rank_sign_bits": rank_sign_bits, "lengths": lengths}


ADAPTER_SCALE = 2.0

def features_of(xp, xb, uq, yp, keep, seq):
    xp = xp * keep[:, None]
    xb = xb * keep[:, None]
    left = jnp.dot(xp.T, uq, precision=lax.Precision.HIGHEST, preferred_element_type=jnp.float32)
    right = jnp.dot(xb.T, yp.astype(jnp.float32), precision=lax.Precision.HIGHEST, preferred_element_type=jnp.float32)
    return jnp.concatenate([left.reshape(-1), right.reshape(-1)]) * (ADAPTER_SCALE / math.sqrt(seq))

def reference(output_gradient, acts, weights, adapter_down_factors, adapter_up_factors, feature_sign_bits, rank_sign_bits, lengths):
    wide = (2 * feature_sign_bits - 1).astype(jnp.bfloat16)
    low = (2 * rank_sign_bits - 1).astype(jnp.float32)
    low_left = low[:, :PROJ].astype(jnp.bfloat16)
    low_right = low[:, PROJ:]
    inv_d = 1.0 / math.sqrt(MODEL_WIDTH)
    inv_r = 1.0 / math.sqrt(ADAPTER_RANK)
    positions = jnp.arange(LEN)

    def one_example(items):
        running_gradient, inputs, length = items
        keep = (positions < length).astype(jnp.float32)
        results = []
        for section_index in reversed(range(SECTION_COUNT)):
            current_input = inputs[section_index]
            update_gradient = jnp.dot(running_gradient, adapter_up_factors[section_index].T, preferred_element_type=jnp.float32).astype(jnp.bfloat16)
            y_proj = (jnp.dot(running_gradient, wide, preferred_element_type=jnp.float32) * inv_d).astype(jnp.bfloat16)
            x_proj = jnp.dot(current_input, wide, preferred_element_type=jnp.float32) * inv_d
            input_down_projected = jnp.dot(current_input, adapter_down_factors[section_index], preferred_element_type=jnp.float32)
            u_proj = jnp.dot(update_gradient, low_left, preferred_element_type=jnp.float32) * inv_r
            x_low = jnp.dot(input_down_projected, low_right, precision=lax.Precision.HIGHEST, preferred_element_type=jnp.float32) * inv_r
            results.append(features_of(x_proj, x_low, u_proj, y_proj, keep, LEN))
            frozen_weight = jnp.dot(running_gradient, weights[section_index].T, preferred_element_type=jnp.float32)
            running_gradient = (frozen_weight + ADAPTER_SCALE * jnp.dot(update_gradient, adapter_down_factors[section_index].T, preferred_element_type=jnp.float32)).astype(jnp.bfloat16)
        return jnp.stack(results[::-1])
    return lax.map(one_example, (output_gradient, acts, lengths))
```

```python
import math

import jax
import jax.numpy as jnp
from jax import lax
from jax.sharding import PartitionSpec as P

ADAPTER_SCALE = 2.0
F32 = jnp.float32
BF16 = jnp.bfloat16


def tn(left, right, **kw):
    return lax.dot_general(left, right, (((0,), (0,)), ((), ())), preferred_element_type=F32, **kw)


def per_device(g, acts, weights, down, up, wide_bits, rank_bits, lengths):
    sections = lax.axis_size("pipe")
    s = lax.axis_index("pipe")
    parts = lax.axis_size("tensor")
    t = lax.axis_index("tensor")
    groups = lax.axis_size("dp")
    d = lax.axis_index("dp")
    count, seq, local = g.shape
    width = local * parts
    rank = up.shape[1]
    proj = wide_bits.shape[1]
    sub = local // groups

    w = weights[0].reshape(local, parts, groups, sub)
    w = lax.dynamic_index_in_dim(w, d, 2, False).reshape(local, parts * sub)
    b_sel = up[0].reshape(rank, parts, groups, sub)
    b_sel = lax.dynamic_index_in_dim(b_sel, d, 2, False).reshape(rank, parts * sub)
    a = down[0]
    b_loc = lax.dynamic_slice_in_dim(up[0], t * local, local, 1)
    wide = lax.dynamic_slice_in_dim(wide_bits, t * local, local, 0)
    wide = (2 * wide - 1).astype(BF16)
    low = (2 * rank_bits - 1).astype(BF16)
    qa, qb = low[:, :proj], low[:, proj:]

    bq = tn(b_loc, qa).astype(BF16)
    here = jnp.concatenate([bq, wide], axis=1)
    mine = jnp.where(s == sections - 1, here, jnp.zeros_like(here))
    up_one = [(i, i + 1) for i in range(sections - 1)]
    right = jnp.concatenate([lax.ppermute(bq, "pipe", up_one), wide], axis=1)
    for k in range(1, sections):
        small = tn(a, right).astype(BF16)
        part = tn(w, right) + ADAPTER_SCALE * tn(b_sel, small)
        whole = lax.psum_scatter(part, "tensor", scatter_dimension=0, tiled=True).astype(BF16)
        block = lax.all_gather(whole, "dp", axis=0, tiled=True)
        mine = mine + lax.ppermute(block, "pipe", [(sections - 1, sections - 1 - k)])
        if k + 1 < sections:
            right = lax.ppermute(block, "pipe", up_one)

    tokens = count * seq
    y_part = jnp.dot(g.reshape(tokens, local), mine, preferred_element_type=F32)
    x = acts[:, 0].reshape(tokens, local)
    xp = jnp.dot(x, wide, preferred_element_type=F32)
    xa = jnp.dot(x, a, preferred_element_type=F32)
    xb = jnp.dot(xa, qb.astype(F32), precision=lax.Precision.HIGHEST, preferred_element_type=F32)
    x_part = jnp.concatenate([xp, xb], axis=1)
    y = lax.psum_scatter(y_part, "tensor", scatter_dimension=0, tiled=True)
    xs = lax.psum_scatter(x_part, "tensor", scatter_dimension=0, tiled=True)
    per = tokens // parts
    index = t * per + jnp.arange(per)
    keep = (index % seq < lengths[index // seq]).astype(F32)[:, None]
    scale = ADAPTER_SCALE / math.sqrt(seq) / math.sqrt(width) / math.sqrt(rank)
    xs = xs * keep * scale
    hi = lax.Precision.HIGHEST
    left = tn(xs[:, :proj], y[:, :proj], precision=hi)
    rite = tn(xs[:, proj:], y[:, proj:], precision=hi)
    full = jnp.concatenate([left.reshape(-1), rite.reshape(-1)]).reshape(parts, -1)
    got = lax.all_to_all(full, "tensor", 0, 0, tiled=True)
    return got.reshape(count, parts // count, -1).sum(1)[:, None, :]


def solution(mesh):
    placed = (
        P("dp", None, "tensor"),
        P("dp", "pipe", None, "tensor"),
        P("pipe", "tensor", None),
        P("pipe", "tensor", None),
        P("pipe", None, None),
        P(),
        P(),
        P("dp"),
    )
    return jax.shard_map(
        per_device, mesh=mesh, in_specs=placed, out_specs=P("dp", "pipe", "tensor"), check_vma=False
    )
```

```python
import functools
import math

import jax
import jax.numpy as jnp
from jax import lax
from jax.experimental import pallas as pl
from jax.experimental.pallas import tpu as pltpu
from jax.sharding import PartitionSpec as P

ADAPTER_SCALE = 2.0
F32 = jnp.float32
BF16 = jnp.bfloat16
MESH = pl.DeviceIdType.MESH
SELF = 5


def dot(left, right):
    return jnp.dot(left, right, preferred_element_type=F32)


def nt(left, right):
    return lax.dot_general(left, right, (((1,), (1,)), ((), ())), preferred_element_type=F32)


def tn(left, right, **kw):
    return lax.dot_general(left, right, (((0,), (0,)), ((), ())), preferred_element_type=F32, **kw)


def identity(rows, cols):
    r = lax.broadcasted_iota(jnp.int32, (rows, cols), 0)
    q = lax.broadcasted_iota(jnp.int32, (rows, cols), 1)
    return jnp.where(r == q, 1.0, 0.0).astype(BF16)


def kernel(
    sizes,
    g_hbm, x_hbm, w_hbm, a_hbm, b_hbm, wide_hbm, rank_hbm, len_ref,
    out_ref,
    g_v, x_v, w_v, a_v, b_own, b_out, wide_v, rank_v,
    vbuf, rt, gbuf, part, parts_in, x_out, x_in, y_out, y_in, f_out, f_in,
    load_sem, rt_send, rt_recv, g_send, g_recv, p_send, p_recv,
    x_send, x_recv, y_send, y_recv, f_send, f_recv,
):
    local, proj, seq = sizes
    half = local // 2
    s = lax.axis_index("pipe")
    d = lax.axis_index("dp")
    t = lax.axis_index("tensor")
    zh, c = d // 2, d % 2
    z, x = t // 4, t % 4

    def peer(j, sign):
        dx, dz = (j // 2 + 2) % 4, 1 - j % 2
        return ((z + dz) % 2) * 4 + (x + sign * dx + 4) % 4

    def load(src, dst, i):
        return pltpu.make_async_copy(src, dst, load_sem.at[i])

    def cols_of(u):
        return pl.ds(pl.multiple_of(u * local + c * half, half), half)

    rows = pl.ds(pl.multiple_of(t * local, local), local)
    get_rank = load(rank_hbm, rank_v, 0)
    get_own = load(b_hbm.at[:, cols_of(t)], b_own, 1)
    get_wide = load(wide_hbm.at[rows, :], wide_v, 2)
    get_a = load(a_hbm, a_v, 3)
    get_x = load(x_hbm, x_v, 4)
    get_g = load(g_hbm, g_v, 5)
    get_b = [load(b_hbm.at[:, cols_of(u)], b_out.at[u], 6 + u) for u in range(8)]
    get_w = [load(w_hbm.at[:, cols_of(u)], w_v.at[u], 14 + u) for u in range(8)]
    for copy in (get_rank, get_own, get_wide, get_a, get_x):
        copy.start()

    barrier = pltpu.get_barrier_semaphore()
    for i in range(1, 8):
        pl.semaphore_signal(barrier, inc=1, device_id={"tensor": (t + i) % 8}, device_id_type=MESH)
    for i in range(1, 16):
        there = {"pipe": (s + i // 4) % 4, "dp": (d + i % 4) % 4}
        pl.semaphore_signal(barrier, inc=1, device_id=there, device_id_type=MESH)

    @pl.when(s >= 1)
    def _():
        for copy in get_w + get_b:
            copy.start()

    get_g.start()

    get_rank.wait()
    low = (2 * rank_v[...] - 1).astype(F32).astype(BF16)
    low_t = nt(identity(128, 128), low).astype(BF16)
    get_own.wait()
    bq_t = dot(low_t[:proj], b_own[...])
    get_wide.wait()
    own = wide_v[pl.ds(pl.multiple_of(c * half, half), half), :]
    p_t = nt(identity(proj, proj), (2 * own - 1).astype(F32).astype(BF16))
    vbuf[0] = jnp.where(zh == 0, bq_t, p_t).astype(BF16)

    pl.semaphore_wait(barrier, 22)

    def to_next(k, core):
        return pltpu.make_async_remote_copy(
            src_ref=vbuf.at[k], dst_ref=rt.at[k, c],
            send_sem=rt_send.at[k, core], recv_sem=rt_recv.at[k, c],
            device_id={"pipe": (s + 1) % 4, "dp": zh * 2 + core}, device_id_type=MESH,
        )

    def to_final(k, i):
        there = {"pipe": 3 - k, "dp": (d + i) % 4}
        return pltpu.make_async_remote_copy(
            src_ref=vbuf.at[k], dst_ref=gbuf.at[c, pl.ds(pl.multiple_of(zh * proj, proj), proj)],
            send_sem=g_send.at[k, i], recv_sem=g_recv.at[d],
            device_id=there, device_id_type=MESH,
        )

    def from_final(src):
        place = gbuf.at[src % 2, pl.ds(pl.multiple_of((src // 2) * proj, proj), proj)]
        return pltpu.make_async_remote_copy(
            src_ref=vbuf.at[0], dst_ref=place, send_sem=g_send.at[0, 0], recv_sem=g_recv.at[src],
            device_id={"pipe": s}, device_id_type=MESH,
        )

    def hand_on(k):
        if k < 3:
            @pl.when((s >= k) & (s < 3))
            def _():
                for core in range(2):
                    to_next(k, core).start()

        @pl.when(s == 3)
        def _():
            for i in range(1 if k == 0 else 0, 4):
                to_final(k, i).start()

    hand_on(0)

    @pl.when(s == 3)
    def _():
        gbuf[c, pl.ds(pl.multiple_of(zh * proj, proj), proj)] = vbuf[0]

    def swap(out, into, send, recv, j):
        to = peer(j, 1)
        return pltpu.make_async_remote_copy(
            src_ref=out.at[to], dst_ref=into.at[t], send_sem=send.at[j], recv_sem=recv.at[t],
            device_id={"tensor": to}, device_id_type=MESH,
        )

    def total(out, into, send, recv):
        acc = out[t].astype(F32)
        for j in range(8):
            if j != SELF:
                src = peer(j, -1)
                pltpu.make_async_remote_copy(
                    src_ref=out.at[0], dst_ref=into.at[src], send_sem=send.at[j], recv_sem=recv.at[src],
                    device_id={"tensor": src}, device_id_type=MESH,
                ).wait_recv()
                acc = acc + into[src].astype(F32)
        return acc

    def spread(out, into, send, recv):
        for j in range(8):
            if j != SELF:
                swap(out, into, send, recv, j).start()

    get_a.wait()
    lane = lax.broadcasted_iota(jnp.int32, (128, 128), 1)
    qb_wide = jnp.where(lane >= proj, low.astype(F32), 0.0).astype(BF16)
    signs = (2 * wide_v[...] - 1).astype(F32).astype(BF16)
    proj_x = (dot(signs, identity(proj, 128)) + dot(a_v[...], qb_wide)).astype(BF16)
    get_x.wait()
    xs = dot(x_v[...], proj_x)
    x_out[...] = xs.reshape(x_out.shape).astype(x_out.dtype)
    spread(x_out, x_in, x_send, x_recv)

    for k in range(1, 4):
        @pl.when(s >= k)
        def _(k=k):
            if k == 1:
                for copy in get_w + get_b:
                    copy.wait()
            for core in range(2):
                pltpu.make_async_remote_copy(
                    src_ref=vbuf.at[k - 1], dst_ref=rt.at[k - 1, core],
                    send_sem=rt_send.at[k - 1, core], recv_sem=rt_recv.at[k - 1, core],
                    device_id={"pipe": s}, device_id_type=MESH,
                ).wait_recv()
            r0, r1 = rt[k - 1, 0], rt[k - 1, 1]
            small = dot(r0, a_v[:half]) + dot(r1, a_v[half:])
            small = (ADAPTER_SCALE * small).astype(BF16)

            def piece(j, carry):
                to = peer(j, 1)
                value = dot(r0, w_v[to, :half]) + dot(r1, w_v[to, half:]) + dot(small, b_out[to])
                part[k - 1, to] = value.astype(BF16)

                @pl.when(j != SELF)
                def _():
                    swap(part.at[k - 1], parts_in.at[k - 1], p_send.at[k - 1], p_recv.at[k - 1], j).start()

                return carry

            lax.fori_loop(0, 8, piece, 0)
            vbuf[k] = total(part.at[k - 1], parts_in.at[k - 1], p_send.at[k - 1], p_recv.at[k - 1]).astype(BF16)

        hand_on(k)

    get_g.wait()
    for i in range(4):
        if i == 0:
            @pl.when(s < 3)
            def _():
                from_final(d).wait_recv()
        else:
            from_final((d + i) % 4).wait_recv()
    ys = nt(g_v[:, :half], gbuf[0]) + nt(g_v[:, half:], gbuf[1])
    y_out[...] = ys.reshape(y_out.shape).astype(y_out.dtype)
    spread(y_out, y_in, y_send, y_recv)
    xt = total(x_out, x_in, x_send, x_recv)
    per = xt.shape[0]
    index = lax.broadcasted_iota(jnp.int32, xt.shape, 0) + (t * per) % seq
    scale = ADAPTER_SCALE / math.sqrt(seq) / math.sqrt(local * 8) / math.sqrt(128)
    xt = jnp.where(index < len_ref[(t * per) // seq], xt * scale, 0.0)
    yt = total(y_out, y_in, y_send, y_recv)
    full = tn(xt, yt, precision=lax.Precision.HIGHEST)
    f_out[...] = full.reshape(f_out.shape)
    spread(f_out, f_in, f_send, f_recv)
    f_in[t] = f_out[t]
    for j in range(8):
        if j != SELF:
            src = peer(j, -1)
            pltpu.make_async_remote_copy(
                src_ref=f_out.at[0], dst_ref=f_in.at[src], send_sem=f_send.at[j], recv_sem=f_recv.at[src],
                device_id={"tensor": src}, device_id_type=MESH,
            ).wait_recv()
    for e in range(4):
        out_ref[e] = f_in[2 * e] + f_in[2 * e + 1]

    for k in range(3):
        @pl.when((s >= k) & (s < 3))
        def _(k=k):
            for core in range(2):
                to_next(k, core).wait_send()

    @pl.when(s == 3)
    def _():
        for k in range(4):
            for i in range(1 if k == 0 else 0, 4):
                to_final(k, i).wait_send()

    for k in range(1, 4):
        @pl.when(s >= k)
        def _(k=k):
            for j in range(8):
                if j != SELF:
                    swap(part.at[k - 1], parts_in.at[k - 1], p_send.at[k - 1], p_recv.at[k - 1], j).wait_send()

    for out, into, send, recv in (
        (x_out, x_in, x_send, x_recv), (y_out, y_in, y_send, y_recv), (f_out, f_in, f_send, f_recv),
    ):
        for j in range(8):
            if j != SELF:
                swap(out, into, send, recv, j).wait_send()


def per_device(g, acts, weights, down, up, wide_bits, rank_bits, lengths):
    t = lax.axis_index("tensor")
    count, seq, local = g.shape
    tokens = count * seq
    rank, width = up.shape[1:]
    proj = wide_bits.shape[1]
    half = local // 2
    per = tokens // 8
    dma = pltpu.SemaphoreType.DMA
    hbm = pl.BlockSpec(memory_space=pl.ANY)
    out = pl.pallas_call(
        functools.partial(kernel, (local, proj, seq)),
        out_shape=jax.ShapeDtypeStruct((count, 16, 128), F32),
        in_specs=[hbm] * 7 + [pl.BlockSpec(memory_space=pltpu.SMEM)],
        out_specs=pl.BlockSpec(memory_space=pltpu.VMEM),
        scratch_shapes=[
            pltpu.VMEM((tokens, local), BF16),
            pltpu.VMEM((tokens, local), BF16),
            pltpu.VMEM((8, local, half), BF16),
            pltpu.VMEM((local, rank), BF16),
            pltpu.VMEM((rank, half), BF16),
            pltpu.VMEM((8, rank, half), BF16),
            pltpu.VMEM((local, proj), jnp.int32),
            pltpu.VMEM((rank, 2 * proj), jnp.int32),
            pltpu.VMEM((4, proj, half), BF16),
            pltpu.VMEM((3, 2, proj, half), BF16),
            pltpu.VMEM((2, 2 * proj, half), BF16),
            pltpu.VMEM((3, 8, proj, half), BF16),
            pltpu.VMEM((3, 8, proj, half), BF16),
            pltpu.VMEM((8, per, 128), F32),
            pltpu.VMEM((8, per, 128), F32),
            pltpu.VMEM((8, per, 128), BF16),
            pltpu.VMEM((8, per, 128), BF16),
            pltpu.VMEM((8, 16, 128), F32),
            pltpu.VMEM((8, 16, 128), F32),
            dma((22,)), dma((3, 2)), dma((3, 2)), dma((4, 4)), dma((4,)),
            dma((3, 8)), dma((3, 8)),
            dma((8,)), dma((8,)), dma((8,)), dma((8,)), dma((8,)), dma((8,)),
        ],
        compiler_params=pltpu.CompilerParams(
            collective_id=0, has_side_effects=True, vmem_limit_bytes=48 * 1024 * 1024
        ),
    )(
        g.reshape(tokens, local), acts.reshape(tokens, local), weights[0], down[0], up[0],
        wide_bits, rank_bits, lengths,
    )
    out = jnp.where(t < 4, out[:, :, :proj], out[:, :, proj:])
    return out.reshape(count, 1, 16 * proj)


def solution(mesh):
    placed = (
        P("dp", None, "tensor"),
        P("dp", "pipe", None, "tensor"),
        P("pipe", "tensor", None),
        P("pipe", "tensor", None),
        P("pipe", None, None),
        P(),
        P(),
        P("dp"),
    )
    return jax.shard_map(
        per_device, mesh=mesh, in_specs=placed, out_specs=P("dp", "pipe", "tensor"), check_vma=False
    )
```

```python
import functools
import math

import jax
import jax.numpy as jnp
from jax import lax
from jax.experimental import pallas as pl
from jax.experimental.pallas import tpu as pltpu
from jax.sharding import PartitionSpec as P

ADAPTER_SCALE = 2.0
F32 = jnp.float32
BF16 = jnp.bfloat16
MESH = pl.DeviceIdType.MESH
SELF = 5
YP, UQ = 0, 1


def dot(left, right):
    return jnp.dot(left, right, preferred_element_type=F32)


def nt(left, right, **kw):
    return lax.dot_general(left, right, (((1,), (1,)), ((), ())), preferred_element_type=F32, **kw)


def identity(n):
    r = lax.broadcasted_iota(jnp.int32, (n, n), 0)
    q = lax.broadcasted_iota(jnp.int32, (n, n), 1)
    return jnp.where(r == q, 1.0, 0.0).astype(BF16)


def signs_of(bits):
    return (2 * bits - 1).astype(F32).astype(BF16)


def kernel(
    sizes,
    g_hbm, x_hbm, w_hbm, a_hbm, b_hbm, wide_hbm, rank_hbm, len_ref,
    out_ref,
    g_v, x_v, w_v, a_v, b_own, b_out, wide_v, rank_v, low_v,
    vbuf, rt, gbuf, part, parts_in, x_out, x_in, y_out, y_in, y_sum, f_out, f_in,
    load_sem, rt_send, rt_recv, g_send, g_recv, p_send, p_recv,
    x_send, x_recv, y_send, y_recv, f_send, f_recv,
):
    local, proj, seq = sizes
    half, cols = local // 2, proj // 2
    s = lax.axis_index("pipe")
    d = lax.axis_index("dp")
    t = lax.axis_index("tensor")
    zh, c = d // 2, d % 2
    z, x = t // 4, t % 4

    def peer(j, sign):
        dx, dz = (j // 2 + 2) % 4, 1 - j % 2
        return ((z + dz) % 2) * 4 + (x + sign * dx + 4) % 4

    def load(src, dst, i):
        return pltpu.make_async_copy(src, dst, load_sem.at[i])

    def cols_of(u):
        return pl.ds(pl.multiple_of(u * local + c * half, half), half)

    block = pl.ds(pl.multiple_of(t * local, local), local)
    my_cols = pl.ds(pl.multiple_of(zh * cols, cols), cols)
    get_rank = load(rank_hbm, rank_v, 0)
    get_own = load(b_hbm.at[:, block], b_own, 1)
    get_wide = load(wide_hbm.at[:, block], wide_v, 2)
    get_a = load(a_hbm, a_v, 3)
    get_x = load(x_hbm, x_v, 4)
    get_g = load(g_hbm, g_v, 5)
    get_b = [load(b_hbm.at[:, cols_of(u)], b_out.at[u], 6 + u) for u in range(8)]
    get_w = [load(w_hbm.at[:, cols_of(u)], w_v.at[u], 14 + u) for u in range(8)]
    for copy in (get_rank, get_own, get_wide, get_a, get_x):
        copy.start()

    barrier = pltpu.get_barrier_semaphore()
    for i in range(1, 16):
        there = {"pipe": (s + i // 4) % 4, "dp": (d + i % 4) % 4}
        pl.semaphore_signal(barrier, inc=1, device_id=there, device_id_type=MESH)
    for i in range(1, 8):
        pl.semaphore_signal(barrier, inc=1, device_id={"tensor": (t + i) % 8}, device_id_type=MESH)

    @pl.when(s >= 1)
    def _():
        for copy in get_w + get_b:
            copy.start()

    get_g.start()

    get_rank.wait()
    low_v[...] = nt(identity(128), signs_of(rank_v[...])).astype(BF16)
    get_own.wait()
    mine = b_own[:, pl.ds(pl.multiple_of(c * half, half), half)]
    vbuf[UQ, 0] = dot(low_v[my_cols], mine).astype(BF16)
    get_wide.wait()
    p_t = signs_of(wide_v[...])

    @pl.when(s >= 1)
    def _():
        few = signs_of(wide_v[my_cols, :])
        rt[YP, 0, 0] = few[:, :half]
        rt[YP, 0, 1] = few[:, half:]

    @pl.when(s == 3)
    def _():
        bq_t = dot(low_v[:proj], b_own[...]).astype(BF16)
        for h in range(2):
            gbuf[YP, h] = p_t[:, h * half : (h + 1) * half]
            gbuf[UQ, h] = bq_t[:, h * half : (h + 1) * half]

    get_a.wait()
    ab_t = nt(low_v[proj:], a_v[...]).astype(BF16)
    get_x.wait()
    for zz, left in ((0, p_t), (1, ab_t)):
        xs = nt(left, x_v[...]).astype(BF16)
        for e in range(4):
            x_out[zz * 4 + e] = xs[:, e * seq : (e + 1) * seq]

    pl.semaphore_wait(barrier, 22)

    def to_next(ch, k, core):
        return pltpu.make_async_remote_copy(
            src_ref=vbuf.at[ch, k], dst_ref=rt.at[ch, k, c],
            send_sem=rt_send.at[ch, k, core], recv_sem=rt_recv.at[ch, k, c],
            device_id={"pipe": (s + 1) % 4, "dp": zh * 2 + core}, device_id_type=MESH,
        )

    def to_final(ch, k, i):
        return pltpu.make_async_remote_copy(
            src_ref=vbuf.at[ch, k], dst_ref=gbuf.at[ch, c, my_cols],
            send_sem=g_send.at[ch, k, i], recv_sem=g_recv.at[ch, d],
            device_id={"pipe": 3 - k, "dp": (d + i) % 4}, device_id_type=MESH,
        )

    def hand_on(ch, k):
        if k < 3:
            @pl.when((s >= k) & (s < 3))
            def _():
                for core in range(2):
                    to_next(ch, k, core).start()
        if k > 0:
            @pl.when(s == 3)
            def _():
                for i in range(4):
                    to_final(ch, k, i).start()

    def swap(out, into, send, recv, j):
        to = peer(j, 1)
        return pltpu.make_async_remote_copy(
            src_ref=out.at[to], dst_ref=into.at[t], send_sem=send.at[j], recv_sem=recv.at[t],
            device_id={"tensor": to}, device_id_type=MESH,
        )

    def total(out, into, send, recv):
        acc = out[t].astype(F32)
        for j in range(8):
            if j != SELF:
                src = peer(j, -1)
                pltpu.make_async_remote_copy(
                    src_ref=out.at[0], dst_ref=into.at[src], send_sem=send.at[j], recv_sem=recv.at[src],
                    device_id={"tensor": src}, device_id_type=MESH,
                ).wait_recv()
                acc = acc + into[src].astype(F32)
        return acc

    hand_on(UQ, 0)
    for j in range(8):
        if j != SELF:
            swap(x_out, x_in, x_send, x_recv, j).start()

    def group(ch, k):
        i = k - 1
        return part.at[ch, i], parts_in.at[ch, i], p_send.at[ch, i], p_recv.at[ch, i]

    def multiply(ch, k):
        i = k - 1
        if ch == UQ or k > 1:
            for core in range(2):
                pltpu.make_async_remote_copy(
                    src_ref=vbuf.at[ch, i], dst_ref=rt.at[ch, i, core],
                    send_sem=rt_send.at[ch, i, core], recv_sem=rt_recv.at[ch, i, core],
                    device_id={"pipe": (s + 1) % 4}, device_id_type=MESH,
                ).wait_recv()
        r0, r1 = rt[ch, i, 0], rt[ch, i, 1]
        small = dot(r0, a_v[:half]) + dot(r1, a_v[half:])
        small = (ADAPTER_SCALE * small).astype(BF16)

        def piece(j, carry):
            to = peer(j, 1)
            value = dot(r0, w_v[to, :half]) + dot(r1, w_v[to, half:]) + dot(small, b_out[to])
            part[ch, i, to] = value.astype(BF16)

            @pl.when(j != SELF)
            def _():
                swap(*group(ch, k), j).start()

            return carry

        lax.fori_loop(0, 8, piece, 0)

    for k in range(1, 4):
        @pl.when(s >= k)
        def _(k=k):
            if k == 1:
                for copy in get_w + get_b:
                    copy.wait()
            for ch in (YP, UQ):
                multiply(ch, k)
            for ch in (YP, UQ):
                vbuf[ch, k] = total(*group(ch, k)).astype(BF16)
                hand_on(ch, k)

    def y_swap(ch, i):
        e = (x + i) % 4
        to = (1 - ch) * 4 + e
        return pltpu.make_async_remote_copy(
            src_ref=y_out.at[to], dst_ref=y_in.at[t], send_sem=y_send.at[ch, i], recv_sem=y_recv.at[t],
            device_id={"tensor": to}, device_id_type=MESH,
        )

    def y_each(ch, act):
        for i in (2, 1, 3):
            act(y_swap(ch, i))

        @pl.when(z == ch)
        def _():
            act(y_swap(ch, 0))

    xt = total(x_out, x_in, x_send, x_recv)
    token = lax.broadcasted_iota(jnp.int32, xt.shape, 1)
    scale = ADAPTER_SCALE / math.sqrt(seq) / math.sqrt(local * 8) / math.sqrt(128)
    xt = jnp.where(token < len_ref[x], xt * scale, 0.0)
    y_sum[...] = jnp.zeros_like(y_sum)

    get_g.wait()
    for ch in (YP, UQ):
        @pl.when(s < 3)
        def _(ch=ch):
            for src in range(4):
                place = gbuf.at[ch, src % 2, pl.ds((src // 2) * cols, cols)]
                pltpu.make_async_remote_copy(
                    src_ref=vbuf.at[ch, 0], dst_ref=place,
                    send_sem=g_send.at[ch, 0, 0], recv_sem=g_recv.at[ch, src],
                    device_id={"pipe": (s + 1) % 4}, device_id_type=MESH,
                ).wait_recv()

        ys = nt(gbuf[ch, 0], g_v[:, :half]) + nt(gbuf[ch, 1], g_v[:, half:])
        ys = ys.astype(BF16)
        for e in range(4):
            y_out[(1 - ch) * 4 + e] = ys[:, e * seq : (e + 1) * seq]
        y_each(ch, lambda copy: copy.start())

    y_sum[:proj] = total(y_out, y_in, y_send.at[0], y_recv)
    f_out[...] = nt(xt, y_sum[...], precision=lax.Precision.HIGHEST).reshape(f_out.shape)

    def f_swap(i):
        to = (x + i) % 4
        return pltpu.make_async_remote_copy(
            src_ref=f_out.at[to], dst_ref=f_in.at[x], send_sem=f_send.at[i], recv_sem=f_recv.at[x],
            device_id={"tensor": z * 4 + to}, device_id_type=MESH,
        )

    for i in (2, 1, 3):
        f_swap(i).start()
    f_in[x] = f_out[x]
    for i in (2, 1, 3):
        src = (x + i) % 4
        pltpu.make_async_remote_copy(
            src_ref=f_out.at[0], dst_ref=f_in.at[src], send_sem=f_send.at[i], recv_sem=f_recv.at[src],
            device_id={"tensor": z * 4 + src}, device_id_type=MESH,
        ).wait_recv()
    out_ref[...] = f_in[...]

    for ch in (YP, UQ):
        for k in range(1 if ch == YP else 0, 3):
            @pl.when((s >= k) & (s < 3))
            def _(ch=ch, k=k):
                for core in range(2):
                    to_next(ch, k, core).wait_send()

        @pl.when(s == 3)
        def _(ch=ch):
            for k in range(1, 4):
                for i in range(4):
                    to_final(ch, k, i).wait_send()

        for k in range(1, 4):
            @pl.when(s >= k)
            def _(ch=ch, k=k):
                for j in range(8):
                    if j != SELF:
                        swap(*group(ch, k), j).wait_send()

        y_each(ch, lambda copy: copy.wait_send())

    for j in range(8):
        if j != SELF:
            swap(x_out, x_in, x_send, x_recv, j).wait_send()
    for i in (2, 1, 3):
        f_swap(i).wait_send()


def per_device(g, acts, weights, down, up, wide_bits, rank_bits, lengths):
    count, seq, local = g.shape
    tokens = count * seq
    rank = up.shape[1]
    proj = wide_bits.shape[1]
    half, cols = local // 2, proj // 2
    dma = pltpu.SemaphoreType.DMA
    hbm = pl.BlockSpec(memory_space=pltpu.HBM)
    out = pl.pallas_call(
        functools.partial(kernel, (local, proj, seq)),
        out_shape=jax.ShapeDtypeStruct((count, 16, 128), F32),
        in_specs=[hbm] * 7 + [pl.BlockSpec(memory_space=pltpu.SMEM)],
        out_specs=pl.BlockSpec(memory_space=pltpu.VMEM),
        scratch_shapes=[
            pltpu.VMEM((tokens, local), BF16),
            pltpu.VMEM((tokens, local), BF16),
            pltpu.VMEM((8, local, half), BF16),
            pltpu.VMEM((local, rank), BF16),
            pltpu.VMEM((rank, local), BF16),
            pltpu.VMEM((8, rank, half), BF16),
            pltpu.VMEM((proj, local), jnp.int32),
            pltpu.VMEM((rank, 2 * proj), jnp.int32),
            pltpu.VMEM((rank, 2 * proj), BF16),
            pltpu.VMEM((2, 4, cols, half), BF16),
            pltpu.VMEM((2, 3, 2, cols, half), BF16),
            pltpu.VMEM((2, 2, proj, half), BF16),
            pltpu.VMEM((2, 3, 8, cols, half), BF16),
            pltpu.VMEM((2, 3, 8, cols, half), BF16),
            pltpu.VMEM((8, proj, seq), BF16),
            pltpu.VMEM((8, proj, seq), BF16),
            pltpu.VMEM((8, proj, seq), BF16),
            pltpu.VMEM((8, proj, seq), BF16),
            pltpu.VMEM((2 * proj, seq), F32),
            pltpu.VMEM((4, 16, 128), F32),
            pltpu.VMEM((4, 16, 128), F32),
            dma((22,)), dma((2, 3, 2)), dma((2, 3, 2)), dma((2, 4, 4)), dma((2, 4)),
            dma((2, 3, 8)), dma((2, 3, 8)),
            dma((8,)), dma((8,)), dma((2, 8)), dma((8,)), dma((4,)), dma((4,)),
        ],
        compiler_params=pltpu.CompilerParams(
            collective_id=0, has_side_effects=True, vmem_limit_bytes=63 * 1024 * 1024
        ),
    )(
        g.reshape(tokens, local), acts.reshape(tokens, local), weights[0], down[0], up[0],
        wide_bits.T, rank_bits, lengths,
    )
    return out[:, :, :proj].reshape(count, 1, 16 * proj)


def solution(mesh):
    placed = (
        P("dp", None, "tensor"),
        P("dp", "pipe", None, "tensor"),
        P("pipe", "tensor", None),
        P("pipe", "tensor", None),
        P("pipe", None, None),
        P(),
        P(),
        P("dp"),
    )
    return jax.shard_map(
        per_device, mesh=mesh, in_specs=placed, out_specs=P("dp", "pipe", "tensor"), check_vma=False
    )
```

```python
import functools
import math

import jax
import jax.numpy as jnp
from jax import lax
from jax.experimental import pallas as pl
from jax.experimental.pallas import tpu as pltpu
from jax.sharding import PartitionSpec as P

ADAPTER_SCALE = 2.0
F32 = jnp.float32
BF16 = jnp.bfloat16
MESH = pl.DeviceIdType.MESH
SELF = 5
YP, UQ = 0, 1


def dot(left, right):
    return jnp.dot(left, right, preferred_element_type=F32)


def nt(left, right, **kw):
    return lax.dot_general(left, right, (((1,), (1,)), ((), ())), preferred_element_type=F32, **kw)


def reorder(n, first):
    r = lax.broadcasted_iota(jnp.int32, (n, n), 0)
    q = lax.broadcasted_iota(jnp.int32, (n, n), 1)
    half = (n - first) // 2
    even = first + 2 * (r - first)
    from_row = jnp.where(r < first, r, jnp.where(r < first + half, even, even - 2 * half + 1))
    return jnp.where(q == from_row, 1.0, 0.0).astype(BF16)


def signs_of(bits):
    return (2 * bits - 1).astype(F32).astype(BF16)


def kernel(
    sizes,
    g_hbm, x_hbm, w_hbm, a_hbm, b_hbm, wide_hbm, rank_hbm, len_ref,
    out_ref,
    g_v, x_v, w_v, a_v, b_own, b_out, wide_v, rank_v, low_v,
    vbuf, rt, gbuf, part, parts_in, x_out, x_in, x_sum, x_use, y_out, y_in, y_sum, f_out, f_in,
    load_sem, rt_send, rt_recv, g_send, g_recv, p_send, p_recv,
    x_send, x_recv, xs_send, xs_recv, y_send, y_recv, f_send, f_recv,
):
    local, proj, seq = sizes
    half, cols = local // 2, proj // 2
    s = lax.axis_index("pipe")
    d = lax.axis_index("dp")
    t = lax.axis_index("tensor")
    zh, c = d // 2, d % 2
    z, x = t // 4, t % 4
    edge = 1 - ((s + 1) % 4) // 2
    home = s + edge * (3 - 2 * s)

    def peer(j, sign):
        dx, dz = (j // 2 + 2) % 4, 1 - j % 2
        return ((z + dz) % 2) * 4 + (x + sign * dx + 4) % 4

    def load(src, dst, i):
        return pltpu.make_async_copy(src, dst, load_sem.at[i])

    def cols_of(u):
        return pl.ds(pl.multiple_of(u * local + c * half, half), half)

    block = pl.ds(pl.multiple_of(t * local, local), local)
    my_cols = pl.ds(pl.multiple_of(zh * cols, cols), cols)
    get_rank = load(rank_hbm, rank_v, 0)
    get_own = load(b_hbm.at[:, block], b_own, 1)
    get_wide = load(wide_hbm.at[:, block], wide_v, 2)
    get_a = load(a_hbm, a_v, 3)
    get_x = load(x_hbm, x_v, 4)
    get_g = load(g_hbm, g_v, 5)
    get_b = [load(b_hbm.at[:, cols_of(u)], b_out.at[u], 6 + u) for u in range(8)]
    get_w = [load(w_hbm.at[:, cols_of(u)], w_v.at[u], 14 + u) for u in range(8)]
    for copy in (get_rank, get_own, get_wide, get_a, get_x):
        copy.start()

    barrier = pltpu.get_barrier_semaphore()
    for i in range(1, 16):
        there = {"pipe": (s + i // 4) % 4, "dp": (d + i % 4) % 4}
        pl.semaphore_signal(barrier, inc=1, device_id=there, device_id_type=MESH)
    for i in range(1, 8):
        pl.semaphore_signal(barrier, inc=1, device_id={"tensor": (t + i) % 8}, device_id_type=MESH)
    for i in range(1, 4):
        there = {"pipe": 3 - s, "tensor": z * 4 + (x + i) % 4}
        pl.semaphore_signal(barrier, inc=1, device_id=there, device_id_type=MESH)

    @pl.when(s >= 1)
    def _():
        for copy in get_w + get_b:
            copy.start()

    get_g.start()

    get_rank.wait()
    low_v[...] = nt(reorder(128, proj), signs_of(rank_v[...])).astype(BF16)
    get_own.wait()
    mine = b_own[:, pl.ds(pl.multiple_of(c * half, half), half)]
    vbuf[UQ, 0] = dot(low_v[my_cols], mine).astype(BF16)
    get_wide.wait()

    @pl.when(s >= 1)
    def _():
        few = signs_of(wide_v[my_cols, :])
        rt[YP, 0, 0] = few[:, :half]
        rt[YP, 0, 1] = few[:, half:]

    @pl.when(s == 0)
    def _():
        p_t = signs_of(wide_v[...])
        gbuf[YP, 0] = p_t[:, :half]
        gbuf[YP, 1] = p_t[:, half:]

    get_a.wait()
    pl.semaphore_wait(barrier, 25)

    def to_next(ch, k, core):
        return pltpu.make_async_remote_copy(
            src_ref=vbuf.at[ch, k], dst_ref=rt.at[ch, k, c],
            send_sem=rt_send.at[ch, k, core], recv_sem=rt_recv.at[ch, k, c],
            device_id={"pipe": (s + 1) % 4, "dp": zh * 2 + core}, device_id_type=MESH,
        )

    def to_final(ch, k, i):
        return pltpu.make_async_remote_copy(
            src_ref=vbuf.at[ch, k], dst_ref=gbuf.at[ch, c, my_cols],
            send_sem=g_send.at[ch, k, i], recv_sem=g_recv.at[ch, d],
            device_id={"pipe": (0, 2, 1, 3)[k], "dp": (d + i) % 4}, device_id_type=MESH,
        )

    def final_order(k):
        return (2, 1, 3) if k == 3 else (2, 1, 3, 0)

    def hand_on(ch, k):
        if k < 3:
            @pl.when((s >= k) & (s < 3))
            def _():
                for core in range(2):
                    to_next(ch, k, core).start()
        if ch == UQ or k > 0:
            @pl.when(s == 3)
            def _():
                if k == 3:
                    gbuf[ch, c, my_cols] = vbuf[ch, k]
                for i in final_order(k):
                    to_final(ch, k, i).start()

    def swap(out, into, send, recv, j):
        to = peer(j, 1)
        return pltpu.make_async_remote_copy(
            src_ref=out.at[to], dst_ref=into.at[t], send_sem=send.at[j], recv_sem=recv.at[t],
            device_id={"tensor": to}, device_id_type=MESH,
        )

    def total(out, into, send, recv):
        acc = out[t].astype(F32)
        for j in range(8):
            if j != SELF:
                src = peer(j, -1)
                pltpu.make_async_remote_copy(
                    src_ref=out.at[0], dst_ref=into.at[src], send_sem=send.at[j], recv_sem=recv.at[src],
                    device_id={"tensor": src}, device_id_type=MESH,
                ).wait_recv()
                acc = acc + into[src].astype(F32)
        return acc

    hand_on(UQ, 0)

    def project_x():
        get_x.wait()
        p_t = dot(reorder(proj, 0), signs_of(wide_v[...])).astype(BF16)
        ab_t = nt(low_v[proj:], a_v[...]).astype(BF16)
        for zz, left in ((0, p_t), (1, ab_t)):
            xs = nt(left, x_v[...]).astype(BF16)
            for e in range(4):
                x_out[zz * 4 + e] = xs[:, e * seq : (e + 1) * seq]
        for j in range(8):
            if j != SELF:
                swap(x_out, x_in, x_send, x_recv, j).start()

    x_cross = pltpu.make_async_remote_copy(
        src_ref=x_sum, dst_ref=x_use, send_sem=xs_send, recv_sem=xs_recv,
        device_id={"pipe": home}, device_id_type=MESH,
    )

    def sum_x():
        x_sum[...] = total(x_out, x_in, x_send, x_recv)

        @pl.when(edge == 1)
        def _():
            x_cross.start()

        @pl.when(edge == 0)
        def _():
            x_use[...] = x_sum[...]

    @pl.when(s == 0)
    def _():
        project_x()
        sum_x()

    def group(ch, k):
        i = k - 1
        return part.at[ch, i], parts_in.at[ch, i], p_send.at[ch, i], p_recv.at[ch, i]

    def multiply(ch, k):
        i = k - 1
        if ch == UQ or k > 1:
            for core in range(2):
                pltpu.make_async_remote_copy(
                    src_ref=vbuf.at[ch, i], dst_ref=rt.at[ch, i, core],
                    send_sem=rt_send.at[ch, i, core], recv_sem=rt_recv.at[ch, i, core],
                    device_id={"pipe": (s + 1) % 4}, device_id_type=MESH,
                ).wait_recv()
        r0, r1 = rt[ch, i, 0], rt[ch, i, 1]
        small = dot(r0, a_v[:half]) + dot(r1, a_v[half:])
        small = (ADAPTER_SCALE * small).astype(BF16)

        for j in range(8):
            to = peer(j, 1)
            value = dot(r0, w_v[to, :half]) + dot(r1, w_v[to, half:]) + dot(small, b_out[to])
            part[ch, i, to] = value.astype(BF16)
            if j != SELF:
                swap(*group(ch, k), j).start()

    for k in range(1, 4):
        @pl.when(s >= k)
        def _(k=k):
            if k == 1:
                for copy in get_w + get_b:
                    copy.wait()
            for ch in (YP, UQ):
                multiply(ch, k)
            for ch in (YP, UQ):
                vbuf[ch, k] = total(*group(ch, k)).astype(BF16)
                hand_on(ch, k)
                if ch == YP and k == 1:
                    project_x()
                if ch == YP and k == 2:
                    sum_x()

    def y_swap(ch, i):
        e = (x + i) % 4
        to = (1 - ch) * 4 + e
        return pltpu.make_async_remote_copy(
            src_ref=y_out.at[to], dst_ref=y_in.at[t], send_sem=y_send.at[ch, i], recv_sem=y_recv.at[t],
            device_id={"tensor": to}, device_id_type=MESH,
        )

    def y_each(ch, act):
        for i in (2, 1, 3):
            act(y_swap(ch, i))

        @pl.when(z == ch)
        def _():
            act(y_swap(ch, 0))

    @pl.when(s == 1)
    def _():
        sum_x()

    @pl.when(edge == 1)
    def _():
        x_cross.wait_recv()

    xt = x_use[...]
    token = lax.broadcasted_iota(jnp.int32, xt.shape, 1)
    scale = ADAPTER_SCALE / math.sqrt(seq) / math.sqrt(local * 8) / math.sqrt(128)
    xt = jnp.where(token < len_ref[x], xt * scale, 0.0)
    y_sum[...] = jnp.zeros_like(y_sum)

    get_g.wait()
    for ch in (YP, UQ):
        def arrived(src, ch=ch):
            place = gbuf.at[ch, src % 2, pl.ds(pl.multiple_of((src // 2) * cols, cols), cols)]
            pltpu.make_async_remote_copy(
                src_ref=vbuf.at[ch, 0], dst_ref=place,
                send_sem=g_send.at[ch, 0, 0], recv_sem=g_recv.at[ch, src],
                device_id={"pipe": (s + 1) % 4}, device_id_type=MESH,
            ).wait_recv()

        @pl.when((s < 3) & (s >= (1 if ch == YP else 0)))
        def _():
            arrived(d)

        @pl.when(s >= (1 if ch == YP else 0))
        def _():
            for i in range(1, 4):
                arrived((d + i) % 4)

        ys = nt(gbuf[ch, 0], g_v[:, :half]) + nt(gbuf[ch, 1], g_v[:, half:])
        ys = ys.astype(BF16)
        for e in range(4):
            y_out[(1 - ch) * 4 + e] = ys[:, e * seq : (e + 1) * seq]
        y_each(ch, lambda copy: copy.start())

    yt = total(y_out, y_in, y_send.at[0], y_recv)
    y_sum[0, :proj] = yt
    y_sum[1, proj:] = yt
    exact = lax.Precision.HIGHEST
    full = nt(xt[:cols], y_sum[0], precision=exact) + nt(xt[cols:], y_sum[1], precision=exact)
    f_out[...] = full.reshape(f_out.shape)

    def f_swap(i):
        to = (x + i) % 4
        return pltpu.make_async_remote_copy(
            src_ref=f_out.at[to], dst_ref=f_in.at[x], send_sem=f_send.at[i], recv_sem=f_recv.at[x],
            device_id={"pipe": home, "tensor": z * 4 + to}, device_id_type=MESH,
        )

    def f_arrived(i):
        src = (x + i) % 4
        pltpu.make_async_remote_copy(
            src_ref=f_out.at[0], dst_ref=f_in.at[src], send_sem=f_send.at[i], recv_sem=f_recv.at[src],
            device_id={"pipe": home, "tensor": z * 4 + (x + 1) % 4}, device_id_type=MESH,
        ).wait_recv()

    for i in (2, 1, 3):
        f_swap(i).start()

    @pl.when(edge == 1)
    def _():
        f_swap(0).start()
        f_arrived(0)

    @pl.when(edge == 0)
    def _():
        f_in[x] = f_out[x]

    for i in (1, 3, 2):
        f_arrived(i)
    out_ref[...] = f_in[...]

    for ch in (YP, UQ):
        for k in range(1 if ch == YP else 0, 3):
            @pl.when((s >= k) & (s < 3))
            def _(ch=ch, k=k):
                for core in range(2):
                    to_next(ch, k, core).wait_send()

        @pl.when(s == 3)
        def _(ch=ch):
            for k in range(1 if ch == YP else 0, 4):
                for i in final_order(k):
                    to_final(ch, k, i).wait_send()

        for k in range(1, 4):
            @pl.when(s >= k)
            def _(ch=ch, k=k):
                for j in range(8):
                    if j != SELF:
                        swap(*group(ch, k), j).wait_send()

        y_each(ch, lambda copy: copy.wait_send())

    for j in range(8):
        if j != SELF:
            swap(x_out, x_in, x_send, x_recv, j).wait_send()
    for i in (2, 1, 3):
        f_swap(i).wait_send()

    @pl.when(edge == 1)
    def _():
        f_swap(0).wait_send()
        x_cross.wait_send()


def per_device(g, acts, weights, down, up, wide_bits, rank_bits, lengths):
    count, seq, local = g.shape
    tokens = count * seq
    rank = up.shape[1]
    proj = wide_bits.shape[1]
    half, cols = local // 2, proj // 2
    dma = pltpu.SemaphoreType.DMA
    hbm = pl.BlockSpec(memory_space=pltpu.HBM)
    out = pl.pallas_call(
        functools.partial(kernel, (local, proj, seq)),
        out_shape=jax.ShapeDtypeStruct((count, 8, 128), F32),
        in_specs=[hbm] * 7 + [pl.BlockSpec(memory_space=pltpu.SMEM)],
        out_specs=pl.BlockSpec(memory_space=pltpu.VMEM),
        scratch_shapes=[
            pltpu.VMEM((tokens, local), BF16),
            pltpu.VMEM((tokens, local), BF16),
            pltpu.VMEM((8, local, half), BF16),
            pltpu.VMEM((local, rank), BF16),
            pltpu.VMEM((rank, local), BF16),
            pltpu.VMEM((8, rank, half), BF16),
            pltpu.VMEM((proj, local), jnp.int32),
            pltpu.VMEM((rank, 2 * proj), jnp.int32),
            pltpu.VMEM((rank, 2 * proj), BF16),
            pltpu.VMEM((2, 4, cols, half), BF16),
            pltpu.VMEM((2, 3, 2, cols, half), BF16),
            pltpu.VMEM((2, 2, proj, half), BF16),
            pltpu.VMEM((2, 3, 8, cols, half), BF16),
            pltpu.VMEM((2, 3, 8, cols, half), BF16),
            pltpu.VMEM((8, proj, seq), BF16),
            pltpu.VMEM((8, proj, seq), BF16),
            pltpu.VMEM((proj, seq), F32),
            pltpu.VMEM((proj, seq), F32),
            pltpu.VMEM((8, proj, seq), BF16),
            pltpu.VMEM((8, proj, seq), BF16),
            pltpu.VMEM((2, 2 * proj, seq), F32),
            pltpu.VMEM((4, 8, 128), F32),
            pltpu.VMEM((4, 8, 128), F32),
            dma((22,)), dma((2, 3, 2)), dma((2, 3, 2)), dma((2, 4, 4)), dma((2, 4)),
            dma((2, 3, 8)), dma((2, 3, 8)),
            dma((8,)), dma((8,)), dma, dma, dma((2, 8)), dma((8,)), dma((4,)), dma((4,)),
        ],
        compiler_params=pltpu.CompilerParams(
            collective_id=0, has_side_effects=True, vmem_limit_bytes=63 * 1024 * 1024
        ),
    )(
        g.reshape(tokens, local), acts.reshape(tokens, local), weights[0], down[0], up[0],
        wide_bits.T, rank_bits, lengths,
    )
    return out.reshape(count, 1, 16 * proj)


def solution(mesh):
    placed = (
        P("dp", None, "tensor"),
        P("dp", "pipe", None, "tensor"),
        P("pipe", "tensor", None),
        P("pipe", "tensor", None),
        P("pipe", None, None),
        P(),
        P(),
        P("dp"),
    )
    return jax.shard_map(
        per_device, mesh=mesh, in_specs=placed, out_specs=P("dp", "pipe", "tensor"), check_vma=False
    )
```

```python
import functools
import math

import jax
import jax.numpy as jnp
from jax import lax
from jax.experimental import pallas as pl
from jax.experimental.pallas import tpu as pltpu
from jax.sharding import PartitionSpec as P

ADAPTER_SCALE = 2.0
F32 = jnp.float32
BF16 = jnp.bfloat16
MESH = pl.DeviceIdType.MESH
SELF = 5
YP, UQ = 0, 1


def dot(left, right):
    return jnp.dot(left, right, preferred_element_type=F32)


def nt(left, right, **kw):
    return lax.dot_general(left, right, (((1,), (1,)), ((), ())), preferred_element_type=F32, **kw)


def reorder(n, first):
    r = lax.broadcasted_iota(jnp.int32, (n, n), 0)
    q = lax.broadcasted_iota(jnp.int32, (n, n), 1)
    half = (n - first) // 2
    even = first + 2 * (r - first)
    from_row = jnp.where(r < first, r, jnp.where(r < first + half, even, even - 2 * half + 1))
    return jnp.where(q == from_row, 1.0, 0.0).astype(BF16)


def signs_of(bits):
    return (2 * bits - 1).astype(F32).astype(BF16)


def kernel(
    sizes,
    g_hbm, x_hbm, w_hbm, a_hbm, b_hbm, wide_hbm, rank_hbm, len_ref,
    out_ref,
    g_v, x_v, w_v, a_v, b_own, b_out, wide_v, rank_v, low_v,
    vbuf, rt, gmid, gbuf, part, parts_in, x_out, x_in, x_sum, x_use, y_out, y_in, y_sum, f_out, f_in,
    load_sem, rt_send, rt_recv, m_send, m_recv, g_send, g_recv, p_send, p_recv,
    x_send, x_recv, xs_send, xs_recv, y_send, y_recv, f_send, f_recv,
):
    local, proj, seq = sizes
    half, cols = local // 2, proj // 2
    s = lax.axis_index("pipe")
    d = lax.axis_index("dp")
    t = lax.axis_index("tensor")
    zh, c = d // 2, d % 2
    z, x = t // 4, t % 4
    edge = 1 - ((s + 1) % 4) // 2
    home = s + edge * (3 - 2 * s)

    def peer(j, sign):
        dx, dz = (j // 2 + 2) % 4, 1 - j % 2
        return ((z + dz) % 2) * 4 + (x + sign * dx + 4) % 4

    def load(src, dst, i):
        return pltpu.make_async_copy(src, dst, load_sem.at[i])

    def cols_of(u):
        return pl.ds(pl.multiple_of(u * local + c * half, half), half)

    block = pl.ds(pl.multiple_of(t * local, local), local)
    my_cols = pl.ds(pl.multiple_of(zh * cols, cols), cols)
    get_rank = load(rank_hbm, rank_v, 0)
    get_own = load(b_hbm.at[:, block], b_own, 1)
    get_wide = load(wide_hbm.at[:, block], wide_v, 2)
    get_a = load(a_hbm, a_v, 3)
    get_x = load(x_hbm, x_v, 4)
    get_g = load(g_hbm, g_v, 5)
    get_b = [load(b_hbm.at[:, cols_of(u)], b_out.at[u], 6 + u) for u in range(8)]
    get_w = [load(w_hbm.at[:, cols_of(u)], w_v.at[u], 14 + u) for u in range(8)]
    for copy in (get_rank, get_own, get_wide, get_a, get_x):
        copy.start()

    barrier = pltpu.get_barrier_semaphore()
    for i in range(1, 4):
        pl.semaphore_signal(barrier, inc=1, device_id={"pipe": (s + i) % 4}, device_id_type=MESH)
        pl.semaphore_signal(barrier, inc=1, device_id={"dp": (d + i) % 4}, device_id_type=MESH)
    for i in (1, 3):
        there = {"pipe": (s + i) % 4, "dp": zh * 2 + 1 - c}
        pl.semaphore_signal(barrier, inc=1, device_id=there, device_id_type=MESH)
    for i in range(1, 8):
        pl.semaphore_signal(barrier, inc=1, device_id={"tensor": (t + i) % 8}, device_id_type=MESH)
    for i in range(1, 4):
        there = {"pipe": 3 - s, "tensor": z * 4 + (x + i) % 4}
        pl.semaphore_signal(barrier, inc=1, device_id=there, device_id_type=MESH)

    @pl.when(s >= 1)
    def _():
        for copy in get_w + get_b:
            copy.start()

    get_g.start()

    get_rank.wait()
    low_v[...] = nt(reorder(128, proj), signs_of(rank_v[...])).astype(BF16)
    get_own.wait()
    mine = b_own[:, pl.ds(pl.multiple_of(c * half, half), half)]
    vbuf[UQ, 0] = dot(low_v[my_cols], mine).astype(BF16)
    get_wide.wait()

    @pl.when(s >= 1)
    def _():
        few = signs_of(wide_v[my_cols, :])
        rt[YP, 0, 0] = few[:, :half]
        rt[YP, 0, 1] = few[:, half:]

    @pl.when(s == 0)
    def _():
        p_t = signs_of(wide_v[...])
        gbuf[YP, 0] = p_t[:, :half]
        gbuf[YP, 1] = p_t[:, half:]

    get_a.wait()
    pl.semaphore_wait(barrier, 18)

    def to_next(ch, k, core):
        return pltpu.make_async_remote_copy(
            src_ref=vbuf.at[ch, k], dst_ref=rt.at[ch, k, c],
            send_sem=rt_send.at[ch, k, core], recv_sem=rt_recv.at[ch, k, c],
            device_id={"pipe": (s + 1) % 4, "dp": zh * 2 + core}, device_id_type=MESH,
        )

    def to_home(ch, k):
        return pltpu.make_async_remote_copy(
            src_ref=vbuf.at[ch, k], dst_ref=gmid.at[ch],
            send_sem=m_send.at[ch, k], recv_sem=m_recv.at[ch],
            device_id={"pipe": (0, 2, 1)[k]}, device_id_type=MESH,
        )

    def to_group(ch, i):
        return pltpu.make_async_remote_copy(
            src_ref=gmid.at[ch], dst_ref=gbuf.at[ch, c, my_cols],
            send_sem=g_send.at[ch, i], recv_sem=g_recv.at[ch, d],
            device_id={"dp": (d + i) % 4}, device_id_type=MESH,
        )

    def to_groups(ch):
        gbuf[ch, c, my_cols] = gmid[ch]
        for i in (2, 1, 3):
            to_group(ch, i).start()

    def hand_on(ch, k):
        if k < 3:
            @pl.when((s >= k) & (s < 3))
            def _():
                for core in range(2):
                    to_next(ch, k, core).start()
        if k == 3:
            gmid[ch] = vbuf[ch, k]
            to_groups(ch)
        elif ch == UQ or k > 0:
            @pl.when(s == 3)
            def _():
                to_home(ch, k).start()

    def swap(out, into, send, recv, j):
        to = peer(j, 1)
        return pltpu.make_async_remote_copy(
            src_ref=out.at[to], dst_ref=into.at[t], send_sem=send.at[j], recv_sem=recv.at[t],
            device_id={"tensor": to}, device_id_type=MESH,
        )

    def total(out, into, send, recv):
        acc = out[t].astype(F32)
        for j in range(8):
            if j != SELF:
                src = peer(j, -1)
                pltpu.make_async_remote_copy(
                    src_ref=out.at[0], dst_ref=into.at[src], send_sem=send.at[j], recv_sem=recv.at[src],
                    device_id={"tensor": src}, device_id_type=MESH,
                ).wait_recv()
                acc = acc + into[src].astype(F32)
        return acc

    hand_on(UQ, 0)

    def project_x():
        get_x.wait()
        p_t = dot(reorder(proj, 0), signs_of(wide_v[...])).astype(BF16)
        ab_t = nt(low_v[proj:], a_v[...]).astype(BF16)
        for zz, left in ((0, p_t), (1, ab_t)):
            xs = nt(left, x_v[...]).astype(BF16)
            for e in range(4):
                x_out[zz * 4 + e] = xs[:, e * seq : (e + 1) * seq]
        for j in range(8):
            if j != SELF:
                swap(x_out, x_in, x_send, x_recv, j).start()

    x_cross = pltpu.make_async_remote_copy(
        src_ref=x_sum, dst_ref=x_use, send_sem=xs_send, recv_sem=xs_recv,
        device_id={"pipe": home}, device_id_type=MESH,
    )

    def sum_x():
        x_sum[...] = total(x_out, x_in, x_send, x_recv)

        @pl.when(edge == 1)
        def _():
            x_cross.start()

        @pl.when(edge == 0)
        def _():
            x_use[...] = x_sum[...]

    @pl.when(s == 0)
    def _():
        project_x()
        sum_x()

    def group(ch, k):
        i = k - 1
        return part.at[ch, i], parts_in.at[ch, i], p_send.at[ch, i], p_recv.at[ch, i]

    def multiply(ch, k):
        i = k - 1
        if ch == UQ or k > 1:
            for core in range(2):
                pltpu.make_async_remote_copy(
                    src_ref=vbuf.at[ch, i], dst_ref=rt.at[ch, i, core],
                    send_sem=rt_send.at[ch, i, core], recv_sem=rt_recv.at[ch, i, core],
                    device_id={"pipe": (s + 1) % 4}, device_id_type=MESH,
                ).wait_recv()
        r0, r1 = rt[ch, i, 0], rt[ch, i, 1]
        small = dot(r0, a_v[:half]) + dot(r1, a_v[half:])
        small = (ADAPTER_SCALE * small).astype(BF16)

        for j in range(8):
            to = peer(j, 1)
            value = dot(r0, w_v[to, :half]) + dot(r1, w_v[to, half:]) + dot(small, b_out[to])
            part[ch, i, to] = value.astype(BF16)
            if j != SELF:
                swap(*group(ch, k), j).start()

    for k in range(1, 4):
        @pl.when(s >= k)
        def _(k=k):
            if k == 1:
                for copy in get_w + get_b:
                    copy.wait()
            for ch in (YP, UQ):
                multiply(ch, k)
            for ch in (YP, UQ):
                vbuf[ch, k] = total(*group(ch, k)).astype(BF16)
                hand_on(ch, k)
                if ch == YP and k == 1:
                    project_x()
                if ch == YP and k == 2:
                    sum_x()

    def y_swap(ch, i):
        e = (x + i) % 4
        to = (1 - ch) * 4 + e
        return pltpu.make_async_remote_copy(
            src_ref=y_out.at[to], dst_ref=y_in.at[t], send_sem=y_send.at[ch, i], recv_sem=y_recv.at[t],
            device_id={"tensor": to}, device_id_type=MESH,
        )

    def y_each(ch, act):
        for i in (2, 1, 3):
            act(y_swap(ch, i))

        @pl.when(z == ch)
        def _():
            act(y_swap(ch, 0))

    @pl.when(s == 1)
    def _():
        sum_x()

    @pl.when(edge == 1)
    def _():
        x_cross.wait_recv()

    xt = x_use[...]
    token = lax.broadcasted_iota(jnp.int32, xt.shape, 1)
    scale = ADAPTER_SCALE / math.sqrt(seq) / math.sqrt(local * 8) / math.sqrt(128)
    xt = jnp.where(token < len_ref[x], xt * scale, 0.0)
    y_sum[...] = jnp.zeros_like(y_sum)

    get_g.wait()
    for ch in (YP, UQ):
        first = 1 if ch == YP else 0

        @pl.when((s < 3) & (s >= first))
        def _(ch=ch):
            pltpu.make_async_remote_copy(
                src_ref=vbuf.at[ch, 0], dst_ref=gmid.at[ch],
                send_sem=m_send.at[ch, 0], recv_sem=m_recv.at[ch],
                device_id={"pipe": (s + 1) % 4}, device_id_type=MESH,
            ).wait_recv()
            to_groups(ch)

        @pl.when(s >= first)
        def _(ch=ch):
            for i in (1, 3, 2):
                src = (d + i) % 4
                place = gbuf.at[ch, src % 2, pl.ds(pl.multiple_of((src // 2) * cols, cols), cols)]
                pltpu.make_async_remote_copy(
                    src_ref=gmid.at[ch], dst_ref=place,
                    send_sem=g_send.at[ch, 0], recv_sem=g_recv.at[ch, src],
                    device_id={"dp": src}, device_id_type=MESH,
                ).wait_recv()

        ys = nt(gbuf[ch, 0], g_v[:, :half]) + nt(gbuf[ch, 1], g_v[:, half:])
        ys = ys.astype(BF16)
        for e in range(4):
            y_out[(1 - ch) * 4 + e] = ys[:, e * seq : (e + 1) * seq]
        y_each(ch, lambda copy: copy.start())

    yt = total(y_out, y_in, y_send.at[0], y_recv)
    y_sum[0, :proj] = yt
    y_sum[1, proj:] = yt
    exact = lax.Precision.HIGHEST
    full = nt(xt[:cols], y_sum[0], precision=exact) + nt(xt[cols:], y_sum[1], precision=exact)
    f_out[...] = full.reshape(f_out.shape)

    def f_swap(i):
        to = (x + i) % 4
        return pltpu.make_async_remote_copy(
            src_ref=f_out.at[to], dst_ref=f_in.at[x], send_sem=f_send.at[i], recv_sem=f_recv.at[x],
            device_id={"pipe": home, "tensor": z * 4 + to}, device_id_type=MESH,
        )

    def f_arrived(i):
        src = (x + i) % 4
        pltpu.make_async_remote_copy(
            src_ref=f_out.at[0], dst_ref=f_in.at[src], send_sem=f_send.at[i], recv_sem=f_recv.at[src],
            device_id={"pipe": home, "tensor": z * 4 + (x + 1) % 4}, device_id_type=MESH,
        ).wait_recv()

    for i in (2, 1, 3):
        f_swap(i).start()

    @pl.when(edge == 1)
    def _():
        f_swap(0).start()
        f_arrived(0)

    @pl.when(edge == 0)
    def _():
        f_in[x] = f_out[x]

    for i in (1, 3, 2):
        f_arrived(i)
    out_ref[...] = f_in[...]

    for ch in (YP, UQ):
        for k in range(1 if ch == YP else 0, 3):
            @pl.when((s >= k) & (s < 3))
            def _(ch=ch, k=k):
                for core in range(2):
                    to_next(ch, k, core).wait_send()

        @pl.when(s == 3)
        def _(ch=ch):
            for k in range(1 if ch == YP else 0, 3):
                to_home(ch, k).wait_send()

        @pl.when(s >= (1 if ch == YP else 0))
        def _(ch=ch):
            for i in (2, 1, 3):
                to_group(ch, i).wait_send()

        for k in range(1, 4):
            @pl.when(s >= k)
            def _(ch=ch, k=k):
                for j in range(8):
                    if j != SELF:
                        swap(*group(ch, k), j).wait_send()

        y_each(ch, lambda copy: copy.wait_send())

    for j in range(8):
        if j != SELF:
            swap(x_out, x_in, x_send, x_recv, j).wait_send()
    for i in (2, 1, 3):
        f_swap(i).wait_send()

    @pl.when(edge == 1)
    def _():
        f_swap(0).wait_send()
        x_cross.wait_send()


def per_device(g, acts, weights, down, up, wide_bits, rank_bits, lengths):
    count, seq, local = g.shape
    tokens = count * seq
    rank = up.shape[1]
    proj = wide_bits.shape[1]
    half, cols = local // 2, proj // 2
    dma = pltpu.SemaphoreType.DMA
    hbm = pl.BlockSpec(memory_space=pltpu.HBM)
    out = pl.pallas_call(
        functools.partial(kernel, (local, proj, seq)),
        out_shape=pltpu.VMEM((count, 8, 128), F32),
        in_specs=[hbm] * 7 + [pl.BlockSpec(memory_space=pltpu.SMEM)],
        out_specs=pl.BlockSpec(memory_space=pltpu.VMEM),
        scratch_shapes=[
            pltpu.VMEM((tokens, local), BF16),
            pltpu.VMEM((tokens, local), BF16),
            pltpu.VMEM((8, local, half), BF16),
            pltpu.VMEM((local, rank), BF16),
            pltpu.VMEM((rank, local), BF16),
            pltpu.VMEM((8, rank, half), BF16),
            pltpu.VMEM((proj, local), jnp.int32),
            pltpu.VMEM((rank, 2 * proj), jnp.int32),
            pltpu.VMEM((rank, 2 * proj), BF16),
            pltpu.VMEM((2, 4, cols, half), BF16),
            pltpu.VMEM((2, 3, 2, cols, half), BF16),
            pltpu.VMEM((2, cols, half), BF16),
            pltpu.VMEM((2, 2, proj, half), BF16),
            pltpu.VMEM((2, 3, 8, cols, half), BF16),
            pltpu.VMEM((2, 3, 8, cols, half), BF16),
            pltpu.VMEM((8, proj, seq), BF16),
            pltpu.VMEM((8, proj, seq), BF16),
            pltpu.VMEM((proj, seq), F32),
            pltpu.VMEM((proj, seq), F32),
            pltpu.VMEM((8, proj, seq), BF16),
            pltpu.VMEM((8, proj, seq), BF16),
            pltpu.VMEM((2, 2 * proj, seq), F32),
            pltpu.VMEM((4, 8, 128), F32),
            pltpu.VMEM((4, 8, 128), F32),
            dma((22,)), dma((2, 3, 2)), dma((2, 3, 2)), dma((2, 3)), dma((2,)), dma((2, 4)), dma((2, 4)),
            dma((2, 3, 8)), dma((2, 3, 8)),
            dma((8,)), dma((8,)), dma, dma, dma((2, 8)), dma((8,)), dma((4,)), dma((4,)),
        ],
        compiler_params=pltpu.CompilerParams(
            collective_id=0, has_side_effects=True, vmem_limit_bytes=63 * 1024 * 1024
        ),
    )(
        g.reshape(tokens, local), acts.reshape(tokens, local), weights[0], down[0], up[0],
        wide_bits.T, rank_bits, lengths,
    )
    return out.reshape(count, 1, 16 * proj)


def solution(mesh):
    placed = (
        P("dp", None, "tensor"),
        P("dp", "pipe", None, "tensor"),
        P("pipe", "tensor", None),
        P("pipe", "tensor", None),
        P("pipe", None, None),
        P(),
        P(),
        P("dp"),
    )
    return jax.shard_map(
        per_device, mesh=mesh, in_specs=placed, out_specs=P("dp", "pipe", "tensor"), check_vma=False
    )
```

```python
import functools
import math

import jax
import jax.numpy as jnp
from jax import lax
from jax.experimental import pallas as pl
from jax.experimental.pallas import tpu as pltpu
from jax.sharding import PartitionSpec as P

ADAPTER_SCALE = 2.0
F32 = jnp.float32
BF16 = jnp.bfloat16
MESH = pl.DeviceIdType.MESH
ORDER = ((2, 1), (2, 0), (1, 1), (3, 1), (1, 0), (3, 0), (0, 1), (0, 0))
SELF = 7
YP, UQ = 0, 1


def dot(left, right):
    return jnp.dot(left, right, preferred_element_type=F32)


def nt(left, right, **kw):
    return lax.dot_general(left, right, (((1,), (1,)), ((), ())), preferred_element_type=F32, **kw)


def reorder(n, first):
    r = lax.broadcasted_iota(jnp.int32, (n, n), 0)
    q = lax.broadcasted_iota(jnp.int32, (n, n), 1)
    half = (n - first) // 2
    even = first + 2 * (r - first)
    from_row = jnp.where(r < first, r, jnp.where(r < first + half, even, even - 2 * half + 1))
    return jnp.where(q == from_row, 1.0, 0.0).astype(BF16)


def signs_of(bits):
    return (2 * bits - 1).astype(F32).astype(BF16)


def kernel(
    sizes,
    g_hbm, x_hbm, w_hbm, a_hbm, b_hbm, wide_hbm, rank_hbm, len_ref,
    out_ref,
    g_v, x_v, w_v, a_v, b_own, b_out, wide_v, rank_v, low_v,
    vbuf, rt, gmid, gbuf, part, parts_in, x_out, x_in, x_sum, x_all, h_v, f_out, f_in,
    load_sem, rt_send, rt_recv, m_send, m_recv, g_send, g_recv, p_send, p_recv,
    x_send, x_recv, xs_send, xs_recv, f_send, f_recv,
):
    local, proj, seq = sizes
    half, cols = local // 2, proj // 2
    s = lax.axis_index("pipe")
    d = lax.axis_index("dp")
    t = lax.axis_index("tensor")
    zh, c = d // 2, d % 2
    z, x = t // 4, t % 4
    edge = 1 - ((s + 1) % 4) // 2
    home = s + edge * (3 - 2 * s)

    def peer(j, sign):
        dx, dz = ORDER[j]
        return ((z + dz) % 2) * 4 + (x + sign * dx + 4) % 4

    def load(src, dst, i):
        return pltpu.make_async_copy(src, dst, load_sem.at[i])

    def cols_of(u):
        return pl.ds(pl.multiple_of(u * local + c * half, half), half)

    block = pl.ds(pl.multiple_of(t * local, local), local)
    my_cols = pl.ds(pl.multiple_of(zh * cols, cols), cols)
    get_rank = load(rank_hbm, rank_v, 0)
    get_own = load(b_hbm.at[:, block], b_own, 1)
    get_wide = load(wide_hbm.at[:, block], wide_v, 2)
    get_a = load(a_hbm, a_v, 3)
    get_x = load(x_hbm, x_v, 4)
    get_g = load(g_hbm, g_v, 5)
    get_b = [load(b_hbm.at[:, cols_of(u)], b_out.at[u], 6 + u) for u in range(8)]
    get_w = [load(w_hbm.at[:, cols_of(u)], w_v.at[u], 14 + u) for u in range(8)]
    for copy in (get_rank, get_own, get_wide, get_a, get_x):
        copy.start()

    barrier = pltpu.get_barrier_semaphore()
    for i in range(1, 4):
        pl.semaphore_signal(barrier, inc=1, device_id={"pipe": (s + i) % 4}, device_id_type=MESH)
        pl.semaphore_signal(barrier, inc=1, device_id={"dp": (d + i) % 4}, device_id_type=MESH)
    for i in (1, 3):
        there = {"pipe": (s + i) % 4, "dp": zh * 2 + 1 - c}
        pl.semaphore_signal(barrier, inc=1, device_id=there, device_id_type=MESH)
    for i in range(1, 8):
        pl.semaphore_signal(barrier, inc=1, device_id={"tensor": (t + i) % 8}, device_id_type=MESH)

    @pl.when(edge == 1)
    def _():
        for i in range(1, 8):
            there = {"pipe": home, "tensor": (t + i) % 8}
            pl.semaphore_signal(barrier, inc=1, device_id=there, device_id_type=MESH)

    @pl.when(s >= 1)
    def _():
        for copy in get_w + get_b:
            copy.start()

    get_g.start()

    get_rank.wait()
    low_v[...] = nt(reorder(128, proj), signs_of(rank_v[...])).astype(BF16)
    get_own.wait()
    mine = b_own[:, pl.ds(pl.multiple_of(c * half, half), half)]
    vbuf[UQ, 0] = dot(low_v[my_cols], mine).astype(BF16)
    get_wide.wait()

    @pl.when(s >= 1)
    def _():
        few = signs_of(wide_v[my_cols, :])
        rt[YP, 0, 0] = few[:, :half]
        rt[YP, 0, 1] = few[:, half:]

    @pl.when(s == 0)
    def _():
        p_t = signs_of(wide_v[...])
        gbuf[YP, 0] = p_t[:, :half]
        gbuf[YP, 1] = p_t[:, half:]

    get_a.wait()
    pl.semaphore_wait(barrier, 15 + 7 * edge)

    def to_next(ch, k, core):
        return pltpu.make_async_remote_copy(
            src_ref=vbuf.at[ch, k], dst_ref=rt.at[ch, k, c],
            send_sem=rt_send.at[ch, k, core], recv_sem=rt_recv.at[ch, k, c],
            device_id={"pipe": (s + 1) % 4, "dp": zh * 2 + core}, device_id_type=MESH,
        )

    def to_home(ch, k):
        return pltpu.make_async_remote_copy(
            src_ref=vbuf.at[ch, k], dst_ref=gmid.at[ch],
            send_sem=m_send.at[ch, k], recv_sem=m_recv.at[ch],
            device_id={"pipe": (0, 2, 1)[k]}, device_id_type=MESH,
        )

    def to_group(ch, i):
        return pltpu.make_async_remote_copy(
            src_ref=gmid.at[ch], dst_ref=gbuf.at[ch, c, my_cols],
            send_sem=g_send.at[ch, i], recv_sem=g_recv.at[ch, d],
            device_id={"dp": (d + i) % 4}, device_id_type=MESH,
        )

    def to_groups(ch):
        gbuf[ch, c, my_cols] = gmid[ch]
        for i in (2, 1, 3):
            to_group(ch, i).start()

    def hand_on(ch, k):
        if k < 3:
            @pl.when((s >= k) & (s < 3))
            def _():
                for core in range(2):
                    to_next(ch, k, core).start()
        if k == 3:
            gmid[ch] = vbuf[ch, k]
            to_groups(ch)
        elif ch == UQ or k > 0:
            @pl.when(s == 3)
            def _():
                to_home(ch, k).start()

    def swap(out, into, send, recv, j):
        to = peer(j, 1)
        return pltpu.make_async_remote_copy(
            src_ref=out.at[to], dst_ref=into.at[t], send_sem=send.at[j], recv_sem=recv.at[t],
            device_id={"tensor": to}, device_id_type=MESH,
        )

    def total(out, into, send, recv):
        acc = out[t].astype(F32)
        for j in range(8):
            if j != SELF:
                src = peer(j, -1)
                pltpu.make_async_remote_copy(
                    src_ref=out.at[0], dst_ref=into.at[src], send_sem=send.at[j], recv_sem=recv.at[src],
                    device_id={"tensor": src}, device_id_type=MESH,
                ).wait_recv()
                acc = acc + into[src].astype(F32)
        return acc

    hand_on(UQ, 0)

    def project_x():
        get_x.wait()
        p_t = dot(reorder(proj, 0), signs_of(wide_v[...])).astype(BF16)
        ab_t = nt(low_v[proj:], a_v[...]).astype(BF16)
        for zz, left in ((0, p_t), (1, ab_t)):
            xs = nt(left, x_v[...]).astype(BF16)
            for e in range(4):
                x_out[zz * 4 + e] = xs[:, e * seq : (e + 1) * seq]
        for j in range(8):
            if j != SELF:
                swap(x_out, x_in, x_send, x_recv, j).start()

    def share_x(i):
        return pltpu.make_async_remote_copy(
            src_ref=x_sum, dst_ref=x_all.at[t], send_sem=xs_send.at[i], recv_sem=xs_recv.at[t],
            device_id={"pipe": home, "tensor": (t + i) % 8}, device_id_type=MESH,
        )

    def sum_x():
        x_sum[...] = total(x_out, x_in, x_send, x_recv).astype(BF16)
        for i in range(1, 8):
            share_x(i).start()

        @pl.when(edge == 1)
        def _():
            share_x(0).start()

        @pl.when(edge == 0)
        def _():
            x_all[t] = x_sum[...]

    def make_h():
        def arrived(i):
            src = (t + i) % 8
            pltpu.make_async_remote_copy(
                src_ref=x_sum, dst_ref=x_all.at[src], send_sem=xs_send.at[i], recv_sem=xs_recv.at[src],
                device_id={"pipe": home, "tensor": (t + 1) % 8}, device_id_type=MESH,
            ).wait_recv()

        for i in range(1, 8):
            arrived(i)

        @pl.when(edge == 1)
        def _():
            arrived(0)

        get_g.wait()
        token = lax.broadcasted_iota(jnp.int32, (proj, seq), 1)
        for e in range(4):
            given = g_v[e * seq : (e + 1) * seq]
            for ch in (YP, UQ):
                xt = x_all[(1 - ch) * 4 + e].astype(F32)
                xt = jnp.where(token < len_ref[e], xt, 0.0).astype(BF16)
                h = dot(xt, given).astype(BF16)
                for q in range(2):
                    h_v[ch, q, e * cols : (e + 1) * cols] = h[q * cols : (q + 1) * cols]

    @pl.when(s == 0)
    def _():
        project_x()
        sum_x()

    def group(ch, k):
        i = k - 1
        return part.at[ch, i], parts_in.at[ch, i], p_send.at[ch, i], p_recv.at[ch, i]

    def multiply(ch, k):
        i = k - 1
        if ch == UQ or k > 1:
            for core in range(2):
                pltpu.make_async_remote_copy(
                    src_ref=vbuf.at[ch, i], dst_ref=rt.at[ch, i, core],
                    send_sem=rt_send.at[ch, i, core], recv_sem=rt_recv.at[ch, i, core],
                    device_id={"pipe": (s + 1) % 4}, device_id_type=MESH,
                ).wait_recv()
        r0, r1 = rt[ch, i, 0], rt[ch, i, 1]
        small = dot(r0, a_v[:half]) + dot(r1, a_v[half:])
        small = (ADAPTER_SCALE * small).astype(BF16)

        for j in range(8):
            to = peer(j, 1)
            value = dot(r0, w_v[to, :half]) + dot(r1, w_v[to, half:]) + dot(small, b_out[to])
            part[ch, i, to] = value.astype(BF16)
            if j != SELF:
                swap(*group(ch, k), j).start()

    for k in range(1, 4):
        @pl.when(s >= k)
        def _(k=k):
            if k == 1:
                for copy in get_w + get_b:
                    copy.wait()
            for ch in (YP, UQ):
                multiply(ch, k)
            for ch in (YP, UQ):
                vbuf[ch, k] = total(*group(ch, k)).astype(BF16)
                hand_on(ch, k)
                if ch == YP and k == 1:
                    project_x()
                if ch == YP and k == 2:
                    sum_x()
                if ch == YP and k == 3:
                    make_h()

    @pl.when(s == 1)
    def _():
        sum_x()

    @pl.when(s < 3)
    def _():
        make_h()

    def f_swap(ch, i):
        to = (x + i) % 4
        return pltpu.make_async_remote_copy(
            src_ref=f_out.at[ch, to], dst_ref=f_in.at[t], send_sem=f_send.at[ch, i], recv_sem=f_recv.at[t],
            device_id={"pipe": home, "tensor": (1 - ch) * 4 + to}, device_id_type=MESH,
        )

    def f_each(ch, act):
        for i in (2, 1, 3):
            act(f_swap(ch, i))

        @pl.when((edge == 1) | (z == ch))
        def _():
            act(f_swap(ch, 0))

    for ch in (YP, UQ):
        first = 1 if ch == YP else 0

        @pl.when((s < 3) & (s >= first))
        def _(ch=ch):
            pltpu.make_async_remote_copy(
                src_ref=vbuf.at[ch, 0], dst_ref=gmid.at[ch],
                send_sem=m_send.at[ch, 0], recv_sem=m_recv.at[ch],
                device_id={"pipe": (s + 1) % 4}, device_id_type=MESH,
            ).wait_recv()
            to_groups(ch)

        @pl.when(s >= first)
        def _(ch=ch):
            for i in (1, 3, 2):
                src = (d + i) % 4
                place = gbuf.at[ch, src % 2, pl.ds(pl.multiple_of((src // 2) * cols, cols), cols)]
                pltpu.make_async_remote_copy(
                    src_ref=gmid.at[ch], dst_ref=place,
                    send_sem=g_send.at[ch, 0], recv_sem=g_recv.at[ch, src],
                    device_id={"dp": src}, device_id_type=MESH,
                ).wait_recv()

        halves = [
            nt(h_v[ch, q, :, :half], gbuf[ch, 0]) + nt(h_v[ch, q, :, half:], gbuf[ch, 1]) for q in range(2)
        ]
        full = jnp.concatenate(halves, axis=1)
        for e in range(4):
            for p in range(4):
                at = e * cols + p * 8
                f_out[ch, p, e] = full[at : at + 8]
        f_each(ch, lambda copy: copy.start())

    def f_arrived(j):
        src = peer(j, -1)
        pltpu.make_async_remote_copy(
            src_ref=f_out.at[0, 0], dst_ref=f_in.at[src], send_sem=f_send.at[0, 0], recv_sem=f_recv.at[src],
            device_id={"pipe": home, "tensor": (t + 1) % 8}, device_id_type=MESH,
        ).wait_recv()
        return f_in[src]

    @pl.when(edge == 1)
    def _():
        f_arrived(SELF)

    @pl.when(edge == 0)
    def _():
        f_in[t] = f_out[1 - z, x]

    acc = f_in[t]
    for j in reversed(range(7)):
        acc = acc + f_arrived(j)
    scale = ADAPTER_SCALE / math.sqrt(seq) / math.sqrt(local * 8) / math.sqrt(128)
    out_ref[...] = acc * scale

    for ch in (YP, UQ):
        for k in range(1 if ch == YP else 0, 3):
            @pl.when((s >= k) & (s < 3))
            def _(ch=ch, k=k):
                for core in range(2):
                    to_next(ch, k, core).wait_send()

        @pl.when(s == 3)
        def _(ch=ch):
            for k in range(1 if ch == YP else 0, 3):
                to_home(ch, k).wait_send()

        @pl.when(s >= (1 if ch == YP else 0))
        def _(ch=ch):
            for i in (2, 1, 3):
                to_group(ch, i).wait_send()

        for k in range(1, 4):
            @pl.when(s >= k)
            def _(ch=ch, k=k):
                for j in range(8):
                    if j != SELF:
                        swap(*group(ch, k), j).wait_send()

        f_each(ch, lambda copy: copy.wait_send())

    for j in range(8):
        if j != SELF:
            swap(x_out, x_in, x_send, x_recv, j).wait_send()
    for i in range(1, 8):
        share_x(i).wait_send()

    @pl.when(edge == 1)
    def _():
        share_x(0).wait_send()


def per_device(g, acts, weights, down, up, wide_bits, rank_bits, lengths):
    count, seq, local = g.shape
    tokens = count * seq
    rank = up.shape[1]
    proj = wide_bits.shape[1]
    half, cols = local // 2, proj // 2
    dma = pltpu.SemaphoreType.DMA
    hbm = pl.BlockSpec(memory_space=pltpu.HBM)
    out = pl.pallas_call(
        functools.partial(kernel, (local, proj, seq)),
        out_shape=pltpu.VMEM((count, 8, 128), F32),
        in_specs=[hbm] * 7 + [pl.BlockSpec(memory_space=pltpu.SMEM)],
        out_specs=pl.BlockSpec(memory_space=pltpu.VMEM),
        scratch_shapes=[
            pltpu.VMEM((tokens, local), BF16),
            pltpu.VMEM((tokens, local), BF16),
            pltpu.VMEM((8, local, half), BF16),
            pltpu.VMEM((local, rank), BF16),
            pltpu.VMEM((rank, local), BF16),
            pltpu.VMEM((8, rank, half), BF16),
            pltpu.VMEM((proj, local), jnp.int32),
            pltpu.VMEM((rank, 2 * proj), jnp.int32),
            pltpu.VMEM((rank, 2 * proj), BF16),
            pltpu.VMEM((2, 4, cols, half), BF16),
            pltpu.VMEM((2, 3, 2, cols, half), BF16),
            pltpu.VMEM((2, cols, half), BF16),
            pltpu.VMEM((2, 2, proj, half), BF16),
            pltpu.VMEM((2, 3, 8, cols, half), BF16),
            pltpu.VMEM((2, 3, 8, cols, half), BF16),
            pltpu.VMEM((8, proj, seq), BF16),
            pltpu.VMEM((8, proj, seq), BF16),
            pltpu.VMEM((proj, seq), BF16),
            pltpu.VMEM((8, proj, seq), BF16),
            pltpu.VMEM((2, 2, 4 * cols, local), BF16),
            pltpu.VMEM((2, 4, 4, 8, 128), F32),
            pltpu.VMEM((8, 4, 8, 128), F32),
            dma((22,)), dma((2, 3, 2)), dma((2, 3, 2)), dma((2, 3)), dma((2,)), dma((2, 4)), dma((2, 4)),
            dma((2, 3, 8)), dma((2, 3, 8)),
            dma((8,)), dma((8,)), dma((8,)), dma((8,)), dma((2, 4)), dma((8,)),
        ],
        compiler_params=pltpu.CompilerParams(
            collective_id=0, has_side_effects=True, vmem_limit_bytes=63 * 1024 * 1024
        ),
    )(
        g.reshape(tokens, local), acts.reshape(tokens, local), weights[0], down[0], up[0],
        wide_bits.T, rank_bits, lengths,
    )
    return out.reshape(count, 1, 16 * proj)


def solution(mesh):
    placed = (
        P("dp", None, "tensor"),
        P("dp", "pipe", None, "tensor"),
        P("pipe", "tensor", None),
        P("pipe", "tensor", None),
        P("pipe", None, None),
        P(),
        P(),
        P("dp"),
    )
    return jax.shard_map(
        per_device, mesh=mesh, in_specs=placed, out_specs=P("dp", "pipe", "tensor"), check_vma=False
    )
```

```python
import functools
import math

import jax
import jax.numpy as jnp
from jax import lax
from jax.experimental import pallas as pl
from jax.experimental.pallas import tpu as pltpu
from jax.sharding import PartitionSpec as P

ADAPTER_SCALE = 2.0
F32 = jnp.float32
BF16 = jnp.bfloat16
MESH = pl.DeviceIdType.MESH
ORDER = ((2, 1), (2, 0), (1, 1), (3, 1), (1, 0), (3, 0), (0, 1), (0, 0))
SELF = 7
YP, UQ = 0, 1


def dot(left, right):
    return jnp.dot(left, right, preferred_element_type=F32)


def nt(left, right, **kw):
    return lax.dot_general(left, right, (((1,), (1,)), ((), ())), preferred_element_type=F32, **kw)


def reorder(n, first):
    r = lax.broadcasted_iota(jnp.int32, (n, n), 0)
    q = lax.broadcasted_iota(jnp.int32, (n, n), 1)
    half = (n - first) // 2
    even = first + 2 * (r - first)
    from_row = jnp.where(r < first, r, jnp.where(r < first + half, even, even - 2 * half + 1))
    return jnp.where(q == from_row, 1.0, 0.0).astype(BF16)


def signs_of(bits):
    return (2 * bits - 1).astype(F32).astype(BF16)


def kernel(
    sizes,
    g_hbm, x_hbm, w_hbm, a_hbm, b_hbm, wide_hbm, rank_hbm, len_ref,
    out_ref,
    g_v, x_v, w_v, a_v, b_own, b_out, wide_v, rank_v, low_v,
    vbuf, rt, gmid, gbuf, part, parts_in, x_out, x_in, x_sum, x_all, h_v, f_out, f_in,
    load_sem, rt_send, rt_recv, m_send, m_recv, g_send, g_recv, p_send, p_recv,
    x_send, x_recv, xs_send, xs_recv, f_send, f_recv,
):
    local, proj, seq = sizes
    half, cols = local // 2, proj // 2
    s = lax.axis_index("pipe")
    d = lax.axis_index("dp")
    t = lax.axis_index("tensor")
    zh, c = d // 2, d % 2
    z, x = t // 4, t % 4
    edge = 1 - ((s + 1) % 4) // 2
    home = s + edge * (3 - 2 * s)

    def peer(j, sign):
        dx, dz = ORDER[j]
        return ((z + dz) % 2) * 4 + (x + sign * dx + 4) % 4

    def load(src, dst, i):
        return pltpu.make_async_copy(src, dst, load_sem.at[i])

    def cols_of(u):
        return pl.ds(pl.multiple_of(u * local + c * half, half), half)

    block = pl.ds(pl.multiple_of(t * local, local), local)
    my_cols = pl.ds(pl.multiple_of(zh * cols, cols), cols)
    get_rank = load(rank_hbm, rank_v, 0)
    get_own = load(b_hbm.at[:, block], b_own, 1)
    get_wide = load(wide_hbm.at[:, block], wide_v, 2)
    get_a = load(a_hbm, a_v, 3)
    get_x = load(x_hbm, x_v, 4)
    get_g = load(g_hbm, g_v, 5)

    def weights_of(j):
        u = peer(j, 1)
        return (
            load(b_hbm.at[:, cols_of(u)], b_out.at[u], 6 + j),
            load(w_hbm.at[:, cols_of(u)], w_v.at[u], 14 + j),
        )

    for copy in (get_rank, get_own, get_wide, get_a):
        copy.start()

    @pl.when(s >= 1)
    def _():
        for j in range(8):
            for copy in weights_of(j):
                copy.start()

    @pl.when(s == 0)
    def _():
        get_x.start()
        get_g.start()

    barrier = pltpu.get_barrier_semaphore()
    for i in range(1, 4):
        pl.semaphore_signal(barrier, inc=1, device_id={"pipe": (s + i) % 4}, device_id_type=MESH)
        pl.semaphore_signal(barrier, inc=1, device_id={"dp": (d + i) % 4}, device_id_type=MESH)
    for i in (1, 3):
        there = {"pipe": (s + i) % 4, "dp": zh * 2 + 1 - c}
        pl.semaphore_signal(barrier, inc=1, device_id=there, device_id_type=MESH)
    for i in range(1, 8):
        pl.semaphore_signal(barrier, inc=1, device_id={"tensor": (t + i) % 8}, device_id_type=MESH)

    for i in range(1, 8):
        there = {"pipe": 3 - s, "tensor": (t + i) % 8}
        pl.semaphore_signal(barrier, inc=1, device_id=there, device_id_type=MESH)

    get_rank.wait()
    low_v[...] = nt(reorder(128, proj), signs_of(rank_v[...])).astype(BF16)
    get_own.wait()
    mine = b_own[:, pl.ds(pl.multiple_of(c * half, half), half)]
    vbuf[UQ, 0] = dot(low_v[my_cols], mine).astype(BF16)
    get_wide.wait()

    @pl.when(s >= 1)
    def _():
        few = signs_of(wide_v[my_cols, :])
        rt[YP, 0, 0] = few[:, :half]
        rt[YP, 0, 1] = few[:, half:]

    @pl.when(s == 0)
    def _():
        p_t = signs_of(wide_v[...])
        gbuf[YP, 0] = p_t[:, :half]
        gbuf[YP, 1] = p_t[:, half:]

    get_a.wait()
    pl.semaphore_wait(barrier, 22)

    def to_next(ch, k, core):
        return pltpu.make_async_remote_copy(
            src_ref=vbuf.at[ch, k], dst_ref=rt.at[ch, k, c],
            send_sem=rt_send.at[ch, k, core], recv_sem=rt_recv.at[ch, k, c],
            device_id={"pipe": (s + 1) % 4, "dp": zh * 2 + core}, device_id_type=MESH,
        )

    def to_home(ch, k):
        return pltpu.make_async_remote_copy(
            src_ref=vbuf.at[ch, k], dst_ref=gmid.at[ch],
            send_sem=m_send.at[ch, k], recv_sem=m_recv.at[ch],
            device_id={"pipe": (0, 2, 1)[k]}, device_id_type=MESH,
        )

    def to_group(ch, i):
        return pltpu.make_async_remote_copy(
            src_ref=gmid.at[ch], dst_ref=gbuf.at[ch, c, my_cols],
            send_sem=g_send.at[ch, i], recv_sem=g_recv.at[ch, d],
            device_id={"dp": (d + i) % 4}, device_id_type=MESH,
        )

    def to_groups(ch):
        gbuf[ch, c, my_cols] = gmid[ch]
        for i in (2, 1, 3):
            to_group(ch, i).start()

    def hand_on(ch, k):
        if k < 3:
            @pl.when((s >= k) & (s < 3))
            def _():
                for core in range(2):
                    to_next(ch, k, core).start()
        if k == 3:
            gmid[ch] = vbuf[ch, k]
            to_groups(ch)
        elif ch == UQ or k > 0:
            @pl.when(s == 3)
            def _():
                to_home(ch, k).start()

    def swap(out, into, send, recv, j):
        to = peer(j, 1)
        return pltpu.make_async_remote_copy(
            src_ref=out.at[to], dst_ref=into.at[t], send_sem=send.at[j], recv_sem=recv.at[t],
            device_id={"tensor": to}, device_id_type=MESH,
        )

    def total(out, into, send, recv):
        acc = out[t].astype(F32)
        for j in range(8):
            if j != SELF:
                src = peer(j, -1)
                pltpu.make_async_remote_copy(
                    src_ref=out.at[0], dst_ref=into.at[src], send_sem=send.at[j], recv_sem=recv.at[src],
                    device_id={"tensor": src}, device_id_type=MESH,
                ).wait_recv()
                acc = acc + into[src].astype(F32)
        return acc

    hand_on(UQ, 0)

    def project_x():
        get_x.wait()
        p_t = dot(reorder(proj, 0), signs_of(wide_v[...])).astype(BF16)
        ab_t = nt(low_v[proj:], a_v[...]).astype(BF16)
        for zz, left in ((0, p_t), (1, ab_t)):
            xs = nt(left, x_v[...]).astype(BF16)
            for e in range(4):
                x_out[zz * 4 + e] = xs[:, e * seq : (e + 1) * seq]
        for j in range(8):
            if j != SELF:
                swap(x_out, x_in, x_send, x_recv, j).start()

    def share_x(i):
        return pltpu.make_async_remote_copy(
            src_ref=x_sum, dst_ref=x_all.at[t], send_sem=xs_send.at[i], recv_sem=xs_recv.at[t],
            device_id={"pipe": home, "tensor": (t + i) % 8}, device_id_type=MESH,
        )

    def sum_x():
        x_sum[...] = total(x_out, x_in, x_send, x_recv).astype(BF16)
        for i in range(1, 8):
            share_x(i).start()

        @pl.when(edge == 1)
        def _():
            share_x(0).start()

        @pl.when(edge == 0)
        def _():
            x_all[t] = x_sum[...]

    def make_h():
        def arrived(i):
            src = (t + i) % 8
            pltpu.make_async_remote_copy(
                src_ref=x_sum, dst_ref=x_all.at[src], send_sem=xs_send.at[i], recv_sem=xs_recv.at[src],
                device_id={"pipe": home, "tensor": (t + 1) % 8}, device_id_type=MESH,
            ).wait_recv()

        for i in range(1, 8):
            arrived(i)

        @pl.when(edge == 1)
        def _():
            arrived(0)

        get_g.wait()
        token = lax.broadcasted_iota(jnp.int32, (proj, seq), 1)
        for e in range(4):
            given = g_v[e * seq : (e + 1) * seq]
            for ch in (YP, UQ):
                xt = x_all[(1 - ch) * 4 + e].astype(F32)
                xt = jnp.where(token < len_ref[e], xt, 0.0).astype(BF16)
                h = dot(xt, given).astype(BF16)
                for q in range(2):
                    h_v[ch, q, e * cols : (e + 1) * cols] = h[q * cols : (q + 1) * cols]

    @pl.when(s == 0)
    def _():
        project_x()
        sum_x()

    def group(ch, k):
        i = k - 1
        return part.at[ch, i], parts_in.at[ch, i], p_send.at[ch, i], p_recv.at[ch, i]

    def multiply(ch, k):
        i = k - 1
        if ch == UQ or k > 1:
            for core in range(2):
                pltpu.make_async_remote_copy(
                    src_ref=vbuf.at[ch, i], dst_ref=rt.at[ch, i, core],
                    send_sem=rt_send.at[ch, i, core], recv_sem=rt_recv.at[ch, i, core],
                    device_id={"pipe": (s + 1) % 4}, device_id_type=MESH,
                ).wait_recv()
        r0, r1 = rt[ch, i, 0], rt[ch, i, 1]
        small = dot(r0, a_v[:half]) + dot(r1, a_v[half:])
        small = (ADAPTER_SCALE * small).astype(BF16)

        for j in range(8):
            to = peer(j, 1)
            if ch == YP and k == 1:
                for copy in weights_of(j):
                    copy.wait()
            value = dot(r0, w_v[to, :half]) + dot(r1, w_v[to, half:]) + dot(small, b_out[to])
            part[ch, i, to] = value.astype(BF16)
            if j != SELF:
                swap(*group(ch, k), j).start()

    for k in range(1, 4):
        @pl.when(s >= k)
        def _(k=k):
            multiply(YP, k)
            if k == 1:
                get_x.start()
                get_g.start()
            multiply(UQ, k)
            for ch in (YP, UQ):
                vbuf[ch, k] = total(*group(ch, k)).astype(BF16)
                hand_on(ch, k)
                if ch == YP and k == 1:
                    project_x()
                if ch == YP and k == 2:
                    sum_x()

                    @pl.when(s == 3)
                    def _():
                        make_h()

    @pl.when(s == 1)
    def _():
        sum_x()

    @pl.when(s < 3)
    def _():
        make_h()

    def f_swap(ch, i):
        to = (x + i) % 4
        return pltpu.make_async_remote_copy(
            src_ref=f_out.at[ch, to], dst_ref=f_in.at[t], send_sem=f_send.at[ch, i], recv_sem=f_recv.at[t],
            device_id={"pipe": home, "tensor": (1 - ch) * 4 + to}, device_id_type=MESH,
        )

    def f_each(ch, act):
        for i in (2, 1, 3):
            act(f_swap(ch, i))

        @pl.when((edge == 1) | (z == ch))
        def _():
            act(f_swap(ch, 0))

    for ch in (YP, UQ):
        first = 1 if ch == YP else 0

        @pl.when((s < 3) & (s >= first))
        def _(ch=ch):
            pltpu.make_async_remote_copy(
                src_ref=vbuf.at[ch, 0], dst_ref=gmid.at[ch],
                send_sem=m_send.at[ch, 0], recv_sem=m_recv.at[ch],
                device_id={"pipe": (s + 1) % 4}, device_id_type=MESH,
            ).wait_recv()
            to_groups(ch)

        @pl.when(s >= first)
        def _(ch=ch):
            for i in (1, 3, 2):
                src = (d + i) % 4
                place = gbuf.at[ch, src % 2, pl.ds(pl.multiple_of((src // 2) * cols, cols), cols)]
                pltpu.make_async_remote_copy(
                    src_ref=gmid.at[ch], dst_ref=place,
                    send_sem=g_send.at[ch, 0], recv_sem=g_recv.at[ch, src],
                    device_id={"dp": src}, device_id_type=MESH,
                ).wait_recv()

        halves = [
            nt(h_v[ch, q, :, :half], gbuf[ch, 0]) + nt(h_v[ch, q, :, half:], gbuf[ch, 1]) for q in range(2)
        ]
        full = jnp.concatenate(halves, axis=1)
        for e in range(4):
            for p in range(4):
                at = e * cols + p * 8
                f_out[ch, p, e] = full[at : at + 8]
        f_each(ch, lambda copy: copy.start())

    def f_arrived(j):
        src = peer(j, -1)
        pltpu.make_async_remote_copy(
            src_ref=f_out.at[0, 0], dst_ref=f_in.at[src], send_sem=f_send.at[0, 0], recv_sem=f_recv.at[src],
            device_id={"pipe": home, "tensor": (t + 1) % 8}, device_id_type=MESH,
        ).wait_recv()
        return f_in[src]

    @pl.when(edge == 1)
    def _():
        f_arrived(SELF)

    @pl.when(edge == 0)
    def _():
        f_in[t] = f_out[1 - z, x]

    acc = f_in[t]
    for j in reversed(range(7)):
        acc = acc + f_arrived(j)
    scale = ADAPTER_SCALE / math.sqrt(seq) / math.sqrt(local * 8) / math.sqrt(128)
    out_ref[...] = acc * scale

    for ch in (YP, UQ):
        for k in range(1 if ch == YP else 0, 3):
            @pl.when((s >= k) & (s < 3))
            def _(ch=ch, k=k):
                for core in range(2):
                    to_next(ch, k, core).wait_send()

        @pl.when(s == 3)
        def _(ch=ch):
            for k in range(1 if ch == YP else 0, 3):
                to_home(ch, k).wait_send()

        @pl.when(s >= (1 if ch == YP else 0))
        def _(ch=ch):
            for i in (2, 1, 3):
                to_group(ch, i).wait_send()

        for k in range(1, 4):
            @pl.when(s >= k)
            def _(ch=ch, k=k):
                for j in range(8):
                    if j != SELF:
                        swap(*group(ch, k), j).wait_send()

        f_each(ch, lambda copy: copy.wait_send())

    for j in range(8):
        if j != SELF:
            swap(x_out, x_in, x_send, x_recv, j).wait_send()
    for i in range(1, 8):
        share_x(i).wait_send()

    @pl.when(edge == 1)
    def _():
        share_x(0).wait_send()


def per_device(g, acts, weights, down, up, wide_bits, rank_bits, lengths):
    count, seq, local = g.shape
    tokens = count * seq
    rank = up.shape[1]
    proj = wide_bits.shape[1]
    half, cols = local // 2, proj // 2
    dma = pltpu.SemaphoreType.DMA
    hbm = pl.BlockSpec(memory_space=pltpu.HBM)
    out = pl.pallas_call(
        functools.partial(kernel, (local, proj, seq)),
        out_shape=pltpu.VMEM((count, 8, 128), F32),
        in_specs=[hbm] * 7 + [pl.BlockSpec(memory_space=pltpu.SMEM)],
        out_specs=pl.BlockSpec(memory_space=pltpu.VMEM),
        scratch_shapes=[
            pltpu.VMEM((tokens, local), BF16),
            pltpu.VMEM((tokens, local), BF16),
            pltpu.VMEM((8, local, half), BF16),
            pltpu.VMEM((local, rank), BF16),
            pltpu.VMEM((rank, local), BF16),
            pltpu.VMEM((8, rank, half), BF16),
            pltpu.VMEM((proj, local), jnp.int32),
            pltpu.VMEM((rank, 2 * proj), jnp.int32),
            pltpu.VMEM((rank, 2 * proj), BF16),
            pltpu.VMEM((2, 4, cols, half), BF16),
            pltpu.VMEM((2, 3, 2, cols, half), BF16),
            pltpu.VMEM((2, cols, half), BF16),
            pltpu.VMEM((2, 2, proj, half), BF16),
            pltpu.VMEM((2, 3, 8, cols, half), BF16),
            pltpu.VMEM((2, 3, 8, cols, half), BF16),
            pltpu.VMEM((8, proj, seq), BF16),
            pltpu.VMEM((8, proj, seq), BF16),
            pltpu.VMEM((proj, seq), BF16),
            pltpu.VMEM((8, proj, seq), BF16),
            pltpu.VMEM((2, 2, 4 * cols, local), BF16),
            pltpu.VMEM((2, 4, 4, 8, 128), F32),
            pltpu.VMEM((8, 4, 8, 128), F32),
            dma((22,)), dma((2, 3, 2)), dma((2, 3, 2)), dma((2, 3)), dma((2,)), dma((2, 4)), dma((2, 4)),
            dma((2, 3, 8)), dma((2, 3, 8)),
            dma((8,)), dma((8,)), dma((8,)), dma((8,)), dma((2, 4)), dma((8,)),
        ],
        compiler_params=pltpu.CompilerParams(
            collective_id=0, has_side_effects=True, vmem_limit_bytes=63 * 1024 * 1024
        ),
    )(
        g.reshape(tokens, local), acts.reshape(tokens, local), weights[0], down[0], up[0],
        wide_bits.T, rank_bits, lengths,
    )
    return out.reshape(count, 1, 16 * proj)


def solution(mesh):
    placed = (
        P("dp", None, "tensor"),
        P("dp", "pipe", None, "tensor"),
        P("pipe", "tensor", None),
        P("pipe", "tensor", None),
        P("pipe", None, None),
        P(),
        P(),
        P("dp"),
    )
    return jax.shard_map(
        per_device, mesh=mesh, in_specs=placed, out_specs=P("dp", "pipe", "tensor"), check_vma=False
    )
```

```python
import functools
import math

import jax
import jax.numpy as jnp
from jax import lax
from jax.experimental import pallas as pl
from jax.experimental.pallas import tpu as pltpu
from jax.sharding import PartitionSpec as P

ADAPTER_SCALE = 2.0
F32 = jnp.float32
BF16 = jnp.bfloat16
MESH = pl.DeviceIdType.MESH
ORDER = ((2, 1), (1, 1), (3, 1), (2, 0), (0, 1), (1, 0), (3, 0), (0, 0))
SELF = 7
YP, UQ = 0, 1


def dot(left, right):
    return jnp.dot(left, right, preferred_element_type=F32)


def nt(left, right, **kw):
    return lax.dot_general(left, right, (((1,), (1,)), ((), ())), preferred_element_type=F32, **kw)


def reorder(n, first):
    r = lax.broadcasted_iota(jnp.int32, (n, n), 0)
    q = lax.broadcasted_iota(jnp.int32, (n, n), 1)
    half = (n - first) // 2
    even = first + 2 * (r - first)
    from_row = jnp.where(r < first, r, jnp.where(r < first + half, even, even - 2 * half + 1))
    return jnp.where(q == from_row, 1.0, 0.0).astype(BF16)


def signs_of(bits):
    return (2 * bits - 1).astype(F32).astype(BF16)


def kernel(
    sizes,
    g_hbm, x_hbm, w_hbm, a_hbm, b_hbm, wide_hbm, rank_hbm, len_ref,
    out_ref,
    g_v, x_v, w_v, a_v, b_own, wide_v, rank_v, low_v,
    vbuf, rt, gmid, gbuf, part, parts_in, x_out, x_in, x_sum, x_all, h_v, f_out, f_in,
    load_sem, rt_send, rt_recv, m_send, m_recv, g_send, g_recv, p_send, p_recv,
    x_send, x_recv, xs_send, xs_recv, f_send, f_recv,
):
    local, proj, seq = sizes
    half, cols = local // 2, proj // 2
    s = lax.axis_index("pipe")
    d = lax.axis_index("dp")
    t = lax.axis_index("tensor")
    zh, c = d // 2, d % 2
    z, x = t // 4, t % 4
    edge = 1 - ((s + 1) % 4) // 2
    home = s + edge * (3 - 2 * s)

    def peer(j, sign):
        dx, dz = ORDER[j]
        return ((z + dz) % 2) * 4 + (x + sign * dx + 4) % 4

    def load(src, dst, i):
        return pltpu.make_async_copy(src, dst, load_sem.at[i])

    def cols_of(u):
        return pl.ds(pl.multiple_of(u * local + c * half, half), half)

    block = pl.ds(pl.multiple_of(t * local, local), local)
    my_cols = pl.ds(pl.multiple_of(zh * cols, cols), cols)
    get_rank = load(rank_hbm, rank_v, 0)
    get_own = load(b_hbm.at[:, block], b_own, 1)
    get_wide = load(wide_hbm.at[:, block], wide_v, 2)
    get_a = load(a_hbm, a_v, 3)
    get_x = load(x_hbm, x_v, 4)
    get_g = load(g_hbm, g_v, 5)

    def weights_of(j):
        u = peer(j, 1)
        return (
            load(b_hbm.at[:, cols_of(u)], w_v.at[u, local:], 6 + j),
            load(w_hbm.at[:, cols_of(u)], w_v.at[u, :local], 14 + j),
        )

    for copy in (get_rank, get_own, get_wide, get_a):
        copy.start()

    @pl.when(s >= 1)
    def _():
        for j in range(8):
            for copy in weights_of(j):
                copy.start()

    @pl.when(s == 0)
    def _():
        get_x.start()
        get_g.start()

    barrier = pltpu.get_barrier_semaphore()
    for i in range(1, 4):
        pl.semaphore_signal(barrier, inc=1, device_id={"pipe": (s + i) % 4}, device_id_type=MESH)
        pl.semaphore_signal(barrier, inc=1, device_id={"dp": (d + i) % 4}, device_id_type=MESH)
    for i in (1, 3):
        there = {"pipe": (s + i) % 4, "dp": zh * 2 + 1 - c}
        pl.semaphore_signal(barrier, inc=1, device_id=there, device_id_type=MESH)
    for i in range(1, 8):
        pl.semaphore_signal(barrier, inc=1, device_id={"tensor": (t + i) % 8}, device_id_type=MESH)

    for i in range(1, 8):
        there = {"pipe": 3 - s, "tensor": (t + i) % 8}
        pl.semaphore_signal(barrier, inc=1, device_id=there, device_id_type=MESH)

    get_rank.wait()
    low_v[...] = nt(reorder(128, proj), signs_of(rank_v[...])).astype(BF16)
    get_own.wait()
    mine = b_own[:, pl.ds(pl.multiple_of(c * half, half), half)]
    vbuf[UQ, 0] = dot(low_v[my_cols], mine).astype(BF16)
    get_wide.wait()

    @pl.when(s >= 1)
    def _():
        few = signs_of(wide_v[my_cols, :])
        rt[YP, 0, 0] = few[:, :half]
        rt[YP, 0, 1] = few[:, half:]

    @pl.when(s == 0)
    def _():
        p_t = signs_of(wide_v[...])
        gbuf[YP, 0] = p_t[:, :half]
        gbuf[YP, 1] = p_t[:, half:]

    get_a.wait()
    pl.semaphore_wait(barrier, 22)

    def to_next(ch, k, core):
        return pltpu.make_async_remote_copy(
            src_ref=vbuf.at[ch, k], dst_ref=rt.at[ch, k, c],
            send_sem=rt_send.at[ch, k, core], recv_sem=rt_recv.at[ch, k, c],
            device_id={"pipe": (s + 1) % 4, "dp": zh * 2 + core}, device_id_type=MESH,
        )

    def to_home(ch, k):
        return pltpu.make_async_remote_copy(
            src_ref=vbuf.at[ch, k], dst_ref=gmid.at[ch],
            send_sem=m_send.at[ch, k], recv_sem=m_recv.at[ch],
            device_id={"pipe": (0, 2, 1)[k]}, device_id_type=MESH,
        )

    def to_group(ch, i):
        return pltpu.make_async_remote_copy(
            src_ref=gmid.at[ch], dst_ref=gbuf.at[ch, c, my_cols],
            send_sem=g_send.at[ch, i], recv_sem=g_recv.at[ch, d],
            device_id={"dp": (d + i) % 4}, device_id_type=MESH,
        )

    def to_groups(ch):
        gbuf[ch, c, my_cols] = gmid[ch]
        for i in (2, 1, 3):
            to_group(ch, i).start()

    def hand_on(ch, k):
        if k < 3:
            @pl.when((s >= k) & (s < 3))
            def _():
                for core in range(2):
                    to_next(ch, k, core).start()
        if k == 3:
            gmid[ch] = vbuf[ch, k]
            to_groups(ch)
        elif ch == UQ or k > 0:
            @pl.when(s == 3)
            def _():
                to_home(ch, k).start()

    def swap(out, into, send, recv, j):
        to = peer(j, 1)
        return pltpu.make_async_remote_copy(
            src_ref=out.at[to], dst_ref=into.at[t], send_sem=send.at[j], recv_sem=recv.at[t],
            device_id={"tensor": to}, device_id_type=MESH,
        )

    def total(out, into, send, recv):
        acc = out[t].astype(F32)
        for j in range(8):
            if j != SELF:
                src = peer(j, -1)
                pltpu.make_async_remote_copy(
                    src_ref=out.at[0], dst_ref=into.at[src], send_sem=send.at[j], recv_sem=recv.at[src],
                    device_id={"tensor": src}, device_id_type=MESH,
                ).wait_recv()
                acc = acc + into[src].astype(F32)
        return acc

    hand_on(UQ, 0)

    def project_x():
        get_x.wait()
        p_t = dot(reorder(proj, 0), signs_of(wide_v[...])).astype(BF16)
        ab_t = nt(low_v[proj:], a_v[...]).astype(BF16)
        for zz, left in ((0, p_t), (1, ab_t)):
            xs = nt(left, x_v[...]).astype(BF16)
            for e in range(4):
                x_out[zz * 4 + e] = xs[:, e * seq : (e + 1) * seq]
        for j in range(8):
            if j != SELF:
                swap(x_out, x_in, x_send, x_recv, j).start()

    def share_x(i):
        return pltpu.make_async_remote_copy(
            src_ref=x_sum, dst_ref=x_all.at[t], send_sem=xs_send.at[i], recv_sem=xs_recv.at[t],
            device_id={"pipe": home, "tensor": (t + i) % 8}, device_id_type=MESH,
        )

    def sum_x():
        x_sum[...] = total(x_out, x_in, x_send, x_recv).astype(BF16)
        for i in range(1, 8):
            share_x(i).start()

        @pl.when(edge == 1)
        def _():
            share_x(0).start()

        @pl.when(edge == 0)
        def _():
            x_all[t] = x_sum[...]

    def make_h():
        def arrived(i):
            src = (t + i) % 8
            pltpu.make_async_remote_copy(
                src_ref=x_sum, dst_ref=x_all.at[src], send_sem=xs_send.at[i], recv_sem=xs_recv.at[src],
                device_id={"pipe": home, "tensor": (t + 1) % 8}, device_id_type=MESH,
            ).wait_recv()

        for i in range(1, 8):
            arrived(i)

        @pl.when(edge == 1)
        def _():
            arrived(0)

        get_g.wait()
        token = lax.broadcasted_iota(jnp.int32, (proj, seq), 1)
        for e in range(4):
            given = g_v[e * seq : (e + 1) * seq]
            for ch in (YP, UQ):
                xt = x_all[(1 - ch) * 4 + e].astype(F32)
                xt = jnp.where(token < len_ref[e], xt, 0.0).astype(BF16)
                h = dot(xt, given).astype(BF16)
                for q in range(2):
                    h_v[ch, q, e * cols : (e + 1) * cols] = h[q * cols : (q + 1) * cols]

    @pl.when(s == 0)
    def _():
        project_x()
        sum_x()

    def group(ch, k):
        i = k - 1
        return part.at[ch, i], parts_in.at[ch, i], p_send.at[ch, i], p_recv.at[ch, i]

    def multiply(ch, k):
        i = k - 1
        if ch == UQ or k > 1:
            for core in range(2):
                pltpu.make_async_remote_copy(
                    src_ref=vbuf.at[ch, i], dst_ref=rt.at[ch, i, core],
                    send_sem=rt_send.at[ch, i, core], recv_sem=rt_recv.at[ch, i, core],
                    device_id={"pipe": (s + 1) % 4}, device_id_type=MESH,
                ).wait_recv()
        r0, r1 = rt[ch, i, 0], rt[ch, i, 1]
        small = dot(r0, a_v[:half]) + dot(r1, a_v[half:])
        small = (ADAPTER_SCALE * small).astype(BF16)
        whole = jnp.concatenate([r0, r1, small], axis=1)

        for j in range(8):
            to = peer(j, 1)
            if ch == YP and k == 1:
                for copy in weights_of(j):
                    copy.wait()
            part[ch, i, to] = dot(whole, w_v[to]).astype(BF16)
            if j != SELF:
                swap(*group(ch, k), j).start()

    for k in range(1, 4):
        @pl.when(s >= k)
        def _(k=k):
            multiply(YP, k)
            if k == 1:
                get_x.start()
                get_g.start()
            multiply(UQ, k)
            for ch in (YP, UQ):
                vbuf[ch, k] = total(*group(ch, k)).astype(BF16)
                hand_on(ch, k)
                if ch == YP and k == 1:
                    project_x()
                if ch == YP and k == 2:
                    sum_x()

                    @pl.when(s == 3)
                    def _():
                        make_h()

    @pl.when(s == 1)
    def _():
        sum_x()

    @pl.when(s < 3)
    def _():
        make_h()

    def f_swap(ch, i):
        to = (x + i) % 4
        return pltpu.make_async_remote_copy(
            src_ref=f_out.at[ch, to], dst_ref=f_in.at[t], send_sem=f_send.at[ch, i], recv_sem=f_recv.at[t],
            device_id={"pipe": home, "tensor": (1 - ch) * 4 + to}, device_id_type=MESH,
        )

    def f_each(ch, act):
        for i in (2, 1, 3):
            act(f_swap(ch, i))

        @pl.when((edge == 1) | (z == ch))
        def _():
            act(f_swap(ch, 0))

    for ch in (YP, UQ):
        first = 1 if ch == YP else 0

        @pl.when((s < 3) & (s >= first))
        def _(ch=ch):
            pltpu.make_async_remote_copy(
                src_ref=vbuf.at[ch, 0], dst_ref=gmid.at[ch],
                send_sem=m_send.at[ch, 0], recv_sem=m_recv.at[ch],
                device_id={"pipe": (s + 1) % 4}, device_id_type=MESH,
            ).wait_recv()
            to_groups(ch)

        @pl.when(s >= first)
        def _(ch=ch):
            for i in (1, 3, 2):
                src = (d + i) % 4
                place = gbuf.at[ch, src % 2, pl.ds(pl.multiple_of((src // 2) * cols, cols), cols)]
                pltpu.make_async_remote_copy(
                    src_ref=gmid.at[ch], dst_ref=place,
                    send_sem=g_send.at[ch, 0], recv_sem=g_recv.at[ch, src],
                    device_id={"dp": src}, device_id_type=MESH,
                ).wait_recv()

        halves = [
            nt(h_v[ch, q, :, :half], gbuf[ch, 0]) + nt(h_v[ch, q, :, half:], gbuf[ch, 1]) for q in range(2)
        ]
        full = jnp.concatenate(halves, axis=1)
        for e in range(4):
            for p in range(4):
                at = e * cols + p * 8
                f_out[ch, p, e] = full[at : at + 8]
        f_each(ch, lambda copy: copy.start())

    def f_arrived(j):
        src = peer(j, -1)
        pltpu.make_async_remote_copy(
            src_ref=f_out.at[0, 0], dst_ref=f_in.at[src], send_sem=f_send.at[0, 0], recv_sem=f_recv.at[src],
            device_id={"pipe": home, "tensor": (t + 1) % 8}, device_id_type=MESH,
        ).wait_recv()
        return f_in[src]

    @pl.when(edge == 1)
    def _():
        f_arrived(SELF)

    @pl.when(edge == 0)
    def _():
        f_in[t] = f_out[1 - z, x]

    acc = f_in[t]
    for j in reversed(range(7)):
        acc = acc + f_arrived(j)
    scale = ADAPTER_SCALE / math.sqrt(seq) / math.sqrt(local * 8) / math.sqrt(128)
    out_ref[...] = acc * scale

    for ch in (YP, UQ):
        for k in range(1 if ch == YP else 0, 3):
            @pl.when((s >= k) & (s < 3))
            def _(ch=ch, k=k):
                for core in range(2):
                    to_next(ch, k, core).wait_send()

        @pl.when(s == 3)
        def _(ch=ch):
            for k in range(1 if ch == YP else 0, 3):
                to_home(ch, k).wait_send()

        @pl.when(s >= (1 if ch == YP else 0))
        def _(ch=ch):
            for i in (2, 1, 3):
                to_group(ch, i).wait_send()

        for k in range(1, 4):
            @pl.when(s >= k)
            def _(ch=ch, k=k):
                for j in range(8):
                    if j != SELF:
                        swap(*group(ch, k), j).wait_send()

        f_each(ch, lambda copy: copy.wait_send())

    for j in range(8):
        if j != SELF:
            swap(x_out, x_in, x_send, x_recv, j).wait_send()
    for i in range(1, 8):
        share_x(i).wait_send()

    @pl.when(edge == 1)
    def _():
        share_x(0).wait_send()


def per_device(g, acts, weights, down, up, wide_bits, rank_bits, lengths):
    count, seq, local = g.shape
    tokens = count * seq
    rank = up.shape[1]
    proj = wide_bits.shape[1]
    half, cols = local // 2, proj // 2
    dma = pltpu.SemaphoreType.DMA
    hbm = pl.BlockSpec(memory_space=pltpu.HBM)
    out = pl.pallas_call(
        functools.partial(kernel, (local, proj, seq)),
        out_shape=pltpu.VMEM((count, 8, 128), F32),
        in_specs=[hbm] * 7 + [pl.BlockSpec(memory_space=pltpu.SMEM)],
        out_specs=pl.BlockSpec(memory_space=pltpu.VMEM),
        scratch_shapes=[
            pltpu.VMEM((tokens, local), BF16),
            pltpu.VMEM((tokens, local), BF16),
            pltpu.VMEM((8, local + rank, half), BF16),
            pltpu.VMEM((local, rank), BF16),
            pltpu.VMEM((rank, local), BF16),
            pltpu.VMEM((proj, local), jnp.int32),
            pltpu.VMEM((rank, 2 * proj), jnp.int32),
            pltpu.VMEM((rank, 2 * proj), BF16),
            pltpu.VMEM((2, 4, cols, half), BF16),
            pltpu.VMEM((2, 3, 2, cols, half), BF16),
            pltpu.VMEM((2, cols, half), BF16),
            pltpu.VMEM((2, 2, proj, half), BF16),
            pltpu.VMEM((2, 3, 8, cols, half), BF16),
            pltpu.VMEM((2, 3, 8, cols, half), BF16),
            pltpu.VMEM((8, proj, seq), BF16),
            pltpu.VMEM((8, proj, seq), BF16),
            pltpu.VMEM((proj, seq), BF16),
            pltpu.VMEM((8, proj, seq), BF16),
            pltpu.VMEM((2, 2, 4 * cols, local), BF16),
            pltpu.VMEM((2, 4, 4, 8, 128), F32),
            pltpu.VMEM((8, 4, 8, 128), F32),
            dma((22,)), dma((2, 3, 2)), dma((2, 3, 2)), dma((2, 3)), dma((2,)), dma((2, 4)), dma((2, 4)),
            dma((2, 3, 8)), dma((2, 3, 8)),
            dma((8,)), dma((8,)), dma((8,)), dma((8,)), dma((2, 4)), dma((8,)),
        ],
        compiler_params=pltpu.CompilerParams(
            collective_id=0, has_side_effects=True, vmem_limit_bytes=63 * 1024 * 1024
        ),
    )(
        g.reshape(tokens, local), acts.reshape(tokens, local), weights[0], down[0], up[0],
        wide_bits.T, rank_bits, lengths,
    )
    return out.reshape(count, 1, 16 * proj)


def solution(mesh):
    placed = (
        P("dp", None, "tensor"),
        P("dp", "pipe", None, "tensor"),
        P("pipe", "tensor", None),
        P("pipe", "tensor", None),
        P("pipe", None, None),
        P(),
        P(),
        P("dp"),
    )
    return jax.shard_map(
        per_device, mesh=mesh, in_specs=placed, out_specs=P("dp", "pipe", "tensor"), check_vma=False
    )
```

```python
import functools
import math

import jax
import jax.numpy as jnp
from jax import lax
from jax.experimental import pallas as pl
from jax.experimental.pallas import tpu as pltpu
from jax.sharding import PartitionSpec as P

ADAPTER_SCALE = 2.0
F32 = jnp.float32
BF16 = jnp.bfloat16
MESH = pl.DeviceIdType.MESH
ORDER = ((2, 1), (1, 1), (3, 1), (0, 1), (2, 0), (1, 0), (3, 0), (0, 0))
SELF = 7
YP, UQ = 0, 1


def dot(left, right):
    return jnp.dot(left, right, preferred_element_type=F32)


def nt(left, right, **kw):
    return lax.dot_general(left, right, (((1,), (1,)), ((), ())), preferred_element_type=F32, **kw)


def reorder(n, first):
    r = lax.broadcasted_iota(jnp.int32, (n, n), 0)
    q = lax.broadcasted_iota(jnp.int32, (n, n), 1)
    half = (n - first) // 2
    even = first + 2 * (r - first)
    from_row = jnp.where(r < first, r, jnp.where(r < first + half, even, even - 2 * half + 1))
    return jnp.where(q == from_row, 1.0, 0.0).astype(BF16)


def signs_of(bits):
    return (2 * bits - 1).astype(F32).astype(BF16)


def kernel(
    sizes,
    g_hbm, x_hbm, w_hbm, a_hbm, b_hbm, wide_hbm, rank_hbm, len_ref,
    out_ref,
    g_v, x_v, w_v, a_v, b_own, wide_v, rank_v, low_v,
    vbuf, rt, gmid, gbuf, part, parts_in, x_out, x_in, x_sum, x_all, h_v, f_out, f_in,
    load_sem, rt_send, rt_recv, m_send, m_recv, g_send, g_recv, p_send, p_recv,
    x_send, x_recv, xs_send, xs_recv, f_send, f_recv,
):
    local, proj, seq = sizes
    half, cols = local // 2, proj // 2
    s = lax.axis_index("pipe")
    d = lax.axis_index("dp")
    t = lax.axis_index("tensor")
    zh, c = d // 2, d % 2
    z, x = t // 4, t % 4
    edge = 1 - ((s + 1) % 4) // 2
    home = s + edge * (3 - 2 * s)

    def peer(j, sign):
        dx, dz = ORDER[j]
        return ((z + dz) % 2) * 4 + (x + sign * dx + 4) % 4

    def load(src, dst, i):
        return pltpu.make_async_copy(src, dst, load_sem.at[i])

    def cols_of(u):
        return pl.ds(pl.multiple_of(u * local + c * half, half), half)

    block = pl.ds(pl.multiple_of(t * local, local), local)
    my_cols = pl.ds(pl.multiple_of(zh * cols, cols), cols)
    get_rank = load(rank_hbm, rank_v, 0)
    get_own = load(b_hbm.at[:, block], b_own, 1)
    get_wide = load(wide_hbm.at[:, block], wide_v, 2)
    get_a = load(a_hbm, a_v, 3)
    get_x = load(x_hbm, x_v, 4)
    get_g = load(g_hbm, g_v, 5)

    def weights_of(j):
        u = peer(j, 1)
        return (
            load(b_hbm.at[:, cols_of(u)], w_v.at[u, local:], 6 + j),
            load(w_hbm.at[:, cols_of(u)], w_v.at[u, :local], 14 + j),
        )

    for copy in (get_rank, get_own, get_wide, get_a):
        copy.start()

    @pl.when(s >= 1)
    def _():
        for j in range(8):
            for copy in weights_of(j):
                copy.start()

    @pl.when(s == 0)
    def _():
        get_x.start()
        get_g.start()

    barrier = pltpu.get_barrier_semaphore()
    for i in range(1, 4):
        pl.semaphore_signal(barrier, inc=1, device_id={"pipe": (s + i) % 4}, device_id_type=MESH)
        pl.semaphore_signal(barrier, inc=1, device_id={"dp": (d + i) % 4}, device_id_type=MESH)
    for i in (1, 3):
        there = {"pipe": (s + i) % 4, "dp": zh * 2 + 1 - c}
        pl.semaphore_signal(barrier, inc=1, device_id=there, device_id_type=MESH)
    for i in range(1, 8):
        pl.semaphore_signal(barrier, inc=1, device_id={"tensor": (t + i) % 8}, device_id_type=MESH)

    for i in range(1, 8):
        there = {"pipe": 3 - s, "tensor": (t + i) % 8}
        pl.semaphore_signal(barrier, inc=1, device_id=there, device_id_type=MESH)

    get_rank.wait()
    low_v[...] = nt(reorder(128, proj), signs_of(rank_v[...])).astype(BF16)
    get_own.wait()
    mine = b_own[:, pl.ds(pl.multiple_of(c * half, half), half)]
    vbuf[UQ, 0] = dot(low_v[my_cols], mine).astype(BF16)
    get_wide.wait()

    @pl.when(s >= 1)
    def _():
        few = signs_of(wide_v[my_cols, :])
        rt[YP, 0, 0] = few[:, :half]
        rt[YP, 0, 1] = few[:, half:]

    @pl.when(s == 0)
    def _():
        p_t = signs_of(wide_v[...])
        gbuf[YP, 0] = p_t[:, :half]
        gbuf[YP, 1] = p_t[:, half:]

    get_a.wait()
    pl.semaphore_wait(barrier, 22)

    def to_next(ch, k, core):
        return pltpu.make_async_remote_copy(
            src_ref=vbuf.at[ch, k], dst_ref=rt.at[ch, k, c],
            send_sem=rt_send.at[ch, k, core], recv_sem=rt_recv.at[ch, k, c],
            device_id={"pipe": (s + 1) % 4, "dp": zh * 2 + core}, device_id_type=MESH,
        )

    def to_home(ch, k):
        return pltpu.make_async_remote_copy(
            src_ref=vbuf.at[ch, k], dst_ref=gmid.at[ch],
            send_sem=m_send.at[ch, k], recv_sem=m_recv.at[ch],
            device_id={"pipe": (0, 2, 1)[k]}, device_id_type=MESH,
        )

    def to_group(ch, i):
        return pltpu.make_async_remote_copy(
            src_ref=gmid.at[ch], dst_ref=gbuf.at[ch, c, my_cols],
            send_sem=g_send.at[ch, i], recv_sem=g_recv.at[ch, d],
            device_id={"dp": (d + i) % 4}, device_id_type=MESH,
        )

    def to_groups(ch):
        gbuf[ch, c, my_cols] = gmid[ch]
        for i in (2, 1, 3):
            to_group(ch, i).start()

    def hand_on(ch, k):
        if k < 3:
            @pl.when((s >= k) & (s < 3))
            def _():
                for core in range(2):
                    to_next(ch, k, core).start()
        if k == 3:
            gmid[ch] = vbuf[ch, k]
            to_groups(ch)
        elif ch == UQ or k > 0:
            @pl.when(s == 3)
            def _():
                to_home(ch, k).start()

    def swap(out, into, send, recv, j):
        to = peer(j, 1)
        return pltpu.make_async_remote_copy(
            src_ref=out.at[to], dst_ref=into.at[t], send_sem=send.at[j], recv_sem=recv.at[t],
            device_id={"tensor": to}, device_id_type=MESH,
        )

    def total(out, into, send, recv):
        acc = out[t].astype(F32)
        for j in range(8):
            if j != SELF:
                src = peer(j, -1)
                pltpu.make_async_remote_copy(
                    src_ref=out.at[0], dst_ref=into.at[src], send_sem=send.at[j], recv_sem=recv.at[src],
                    device_id={"tensor": src}, device_id_type=MESH,
                ).wait_recv()
                acc = acc + into[src].astype(F32)
        return acc

    hand_on(UQ, 0)

    def project_x():
        get_x.wait()
        p_t = dot(reorder(proj, 0), signs_of(wide_v[...])).astype(BF16)
        ab_t = nt(low_v[proj:], a_v[...]).astype(BF16)
        for zz, left in ((0, p_t), (1, ab_t)):
            xs = nt(left, x_v[...]).astype(BF16)
            for e in range(4):
                x_out[zz * 4 + e] = xs[:, e * seq : (e + 1) * seq]
        for j in range(8):
            if j != SELF:
                swap(x_out, x_in, x_send, x_recv, j).start()

    def share_x(i):
        return pltpu.make_async_remote_copy(
            src_ref=x_sum, dst_ref=x_all.at[t], send_sem=xs_send.at[i], recv_sem=xs_recv.at[t],
            device_id={"pipe": home, "tensor": (t + i) % 8}, device_id_type=MESH,
        )

    def sum_x():
        x_sum[...] = total(x_out, x_in, x_send, x_recv).astype(BF16)
        for i in range(1, 8):
            share_x(i).start()

        @pl.when(edge == 1)
        def _():
            share_x(0).start()

        @pl.when(edge == 0)
        def _():
            x_all[t] = x_sum[...]

    def make_h():
        def arrived(i):
            src = (t + i) % 8
            pltpu.make_async_remote_copy(
                src_ref=x_sum, dst_ref=x_all.at[src], send_sem=xs_send.at[i], recv_sem=xs_recv.at[src],
                device_id={"pipe": home, "tensor": (t + 1) % 8}, device_id_type=MESH,
            ).wait_recv()

        for i in range(1, 8):
            arrived(i)

        @pl.when(edge == 1)
        def _():
            arrived(0)

        get_g.wait()
        token = lax.broadcasted_iota(jnp.int32, (proj, seq), 1)
        for e in range(4):
            given = g_v[e * seq : (e + 1) * seq]
            for ch in (YP, UQ):
                xt = x_all[(1 - ch) * 4 + e].astype(F32)
                xt = jnp.where(token < len_ref[e], xt, 0.0).astype(BF16)
                h = dot(xt, given).astype(BF16)
                for q in range(2):
                    h_v[ch, q, e * cols : (e + 1) * cols] = h[q * cols : (q + 1) * cols]

    @pl.when(s == 0)
    def _():
        project_x()
        sum_x()

    def group(ch, k):
        i = k - 1
        return part.at[ch, i], parts_in.at[ch, i], p_send.at[ch, i], p_recv.at[ch, i]

    def multiply(ch, k):
        i = k - 1
        if ch == UQ or k > 1:
            for core in range(2):
                pltpu.make_async_remote_copy(
                    src_ref=vbuf.at[ch, i], dst_ref=rt.at[ch, i, core],
                    send_sem=rt_send.at[ch, i, core], recv_sem=rt_recv.at[ch, i, core],
                    device_id={"pipe": (s + 1) % 4}, device_id_type=MESH,
                ).wait_recv()
        r0, r1 = rt[ch, i, 0], rt[ch, i, 1]
        small = dot(r0, a_v[:half]) + dot(r1, a_v[half:])
        small = (ADAPTER_SCALE * small).astype(BF16)
        whole = jnp.concatenate([r0, r1, small], axis=1)

        for j in range(8):
            to = peer(j, 1)
            if ch == YP and k == 1:
                for copy in weights_of(j):
                    copy.wait()
            part[ch, i, to] = dot(whole, w_v[to]).astype(BF16)
            if j != SELF:
                swap(*group(ch, k), j).start()

    for k in range(1, 4):
        @pl.when(s >= k)
        def _(k=k):
            multiply(YP, k)
            if k == 1:
                get_x.start()
                get_g.start()
            multiply(UQ, k)
            for ch in (YP, UQ):
                vbuf[ch, k] = total(*group(ch, k)).astype(BF16)
                hand_on(ch, k)
                if ch == YP and k == 1:
                    project_x()
                if ch == YP and k == 2:
                    sum_x()

                    @pl.when(s == 3)
                    def _():
                        make_h()

    @pl.when(s == 1)
    def _():
        sum_x()

    @pl.when(s < 3)
    def _():
        make_h()

    def f_swap(ch, i):
        to = (x + i) % 4
        return pltpu.make_async_remote_copy(
            src_ref=f_out.at[ch, to], dst_ref=f_in.at[t], send_sem=f_send.at[ch, i], recv_sem=f_recv.at[t],
            device_id={"pipe": home, "tensor": (1 - ch) * 4 + to}, device_id_type=MESH,
        )

    def f_each(ch, act):
        for i in (2, 1, 3):
            act(f_swap(ch, i))

        @pl.when((edge == 1) | (z == ch))
        def _():
            act(f_swap(ch, 0))

    for ch in (YP, UQ):
        first = 1 if ch == YP else 0

        @pl.when((s < 3) & (s >= first))
        def _(ch=ch):
            pltpu.make_async_remote_copy(
                src_ref=vbuf.at[ch, 0], dst_ref=gmid.at[ch],
                send_sem=m_send.at[ch, 0], recv_sem=m_recv.at[ch],
                device_id={"pipe": (s + 1) % 4}, device_id_type=MESH,
            ).wait_recv()
            to_groups(ch)

        @pl.when(s >= first)
        def _(ch=ch):
            for i in (1, 3, 2):
                src = (d + i) % 4
                place = gbuf.at[ch, src % 2, pl.ds(pl.multiple_of((src // 2) * cols, cols), cols)]
                pltpu.make_async_remote_copy(
                    src_ref=gmid.at[ch], dst_ref=place,
                    send_sem=g_send.at[ch, 0], recv_sem=g_recv.at[ch, src],
                    device_id={"dp": src}, device_id_type=MESH,
                ).wait_recv()

        halves = [
            nt(h_v[ch, q, :, :half], gbuf[ch, 0]) + nt(h_v[ch, q, :, half:], gbuf[ch, 1]) for q in range(2)
        ]
        full = jnp.concatenate(halves, axis=1)
        for e in range(4):
            for p in range(4):
                at = e * cols + p * 8
                f_out[ch, p, e] = full[at : at + 8]
        f_each(ch, lambda copy: copy.start())

    def f_arrived(j):
        src = peer(j, -1)
        pltpu.make_async_remote_copy(
            src_ref=f_out.at[0, 0], dst_ref=f_in.at[src], send_sem=f_send.at[0, 0], recv_sem=f_recv.at[src],
            device_id={"pipe": home, "tensor": (t + 1) % 8}, device_id_type=MESH,
        ).wait_recv()
        return f_in[src]

    @pl.when(edge == 1)
    def _():
        f_arrived(SELF)

    @pl.when(edge == 0)
    def _():
        f_in[t] = f_out[1 - z, x]

    acc = f_in[t]
    for j in reversed(range(7)):
        acc = acc + f_arrived(j)
    scale = ADAPTER_SCALE / math.sqrt(seq) / math.sqrt(local * 8) / math.sqrt(128)
    out_ref[...] = acc * scale

    for ch in (YP, UQ):
        for k in range(1 if ch == YP else 0, 3):
            @pl.when((s >= k) & (s < 3))
            def _(ch=ch, k=k):
                for core in range(2):
                    to_next(ch, k, core).wait_send()

        @pl.when(s == 3)
        def _(ch=ch):
            for k in range(1 if ch == YP else 0, 3):
                to_home(ch, k).wait_send()

        @pl.when(s >= (1 if ch == YP else 0))
        def _(ch=ch):
            for i in (2, 1, 3):
                to_group(ch, i).wait_send()

        for k in range(1, 4):
            @pl.when(s >= k)
            def _(ch=ch, k=k):
                for j in range(8):
                    if j != SELF:
                        swap(*group(ch, k), j).wait_send()

        f_each(ch, lambda copy: copy.wait_send())

    for j in range(8):
        if j != SELF:
            swap(x_out, x_in, x_send, x_recv, j).wait_send()
    for i in range(1, 8):
        share_x(i).wait_send()

    @pl.when(edge == 1)
    def _():
        share_x(0).wait_send()


def per_device(g, acts, weights, down, up, wide_bits, rank_bits, lengths):
    count, seq, local = g.shape
    tokens = count * seq
    rank = up.shape[1]
    proj = wide_bits.shape[1]
    half, cols = local // 2, proj // 2
    dma = pltpu.SemaphoreType.DMA
    hbm = pl.BlockSpec(memory_space=pltpu.HBM)
    out = pl.pallas_call(
        functools.partial(kernel, (local, proj, seq)),
        out_shape=pltpu.VMEM((count, 8, 128), F32),
        in_specs=[hbm] * 7 + [pl.BlockSpec(memory_space=pltpu.SMEM)],
        out_specs=pl.BlockSpec(memory_space=pltpu.VMEM),
        scratch_shapes=[
            pltpu.VMEM((tokens, local), BF16),
            pltpu.VMEM((tokens, local), BF16),
            pltpu.VMEM((8, local + rank, half), BF16),
            pltpu.VMEM((local, rank), BF16),
            pltpu.VMEM((rank, local), BF16),
            pltpu.VMEM((proj, local), jnp.int32),
            pltpu.VMEM((rank, 2 * proj), jnp.int32),
            pltpu.VMEM((rank, 2 * proj), BF16),
            pltpu.VMEM((2, 4, cols, half), BF16),
            pltpu.VMEM((2, 3, 2, cols, half), BF16),
            pltpu.VMEM((2, cols, half), BF16),
            pltpu.VMEM((2, 2, proj, half), BF16),
            pltpu.VMEM((2, 3, 8, cols, half), BF16),
            pltpu.VMEM((2, 3, 8, cols, half), BF16),
            pltpu.VMEM((8, proj, seq), BF16),
            pltpu.VMEM((8, proj, seq), BF16),
            pltpu.VMEM((proj, seq), BF16),
            pltpu.VMEM((8, proj, seq), BF16),
            pltpu.VMEM((2, 2, 4 * cols, local), BF16),
            pltpu.VMEM((2, 4, 4, 8, 128), F32),
            pltpu.VMEM((8, 4, 8, 128), F32),
            dma((22,)), dma((2, 3, 2)), dma((2, 3, 2)), dma((2, 3)), dma((2,)), dma((2, 4)), dma((2, 4)),
            dma((2, 3, 8)), dma((2, 3, 8)),
            dma((8,)), dma((8,)), dma((8,)), dma((8,)), dma((2, 4)), dma((8,)),
        ],
        compiler_params=pltpu.CompilerParams(
            collective_id=0, has_side_effects=True, vmem_limit_bytes=63 * 1024 * 1024
        ),
    )(
        g.reshape(tokens, local), acts.reshape(tokens, local), weights[0], down[0], up[0],
        wide_bits.T, rank_bits, lengths,
    )
    return out.reshape(count, 1, 16 * proj)


def solution(mesh):
    placed = (
        P("dp", None, "tensor"),
        P("dp", "pipe", None, "tensor"),
        P("pipe", "tensor", None),
        P("pipe", "tensor", None),
        P("pipe", None, None),
        P(),
        P(),
        P("dp"),
    )
    return jax.shard_map(
        per_device, mesh=mesh, in_specs=placed, out_specs=P("dp", "pipe", "tensor"), check_vma=False
    )
```
